256 devices in a mesh: grp: 8 (over y_lo, x), dev: 32 (over y_hi, z, core).
Axes of the slice: x: 4, y: 4 (y_hi: 2, y_lo: 2; y = y_hi * 2 + y_lo), z: 8, core: 2. Of those that a mesh axis runs over, the one named last changes fastest.
Arguments:
- noise_draws: bfloat16 [16384, 1024], P('dev', 'grp'), may hold values from -12 to 12
- latents: bfloat16 [16384, 1024], P(('grp', 'dev')), may hold values from -6 to 6
Outputs:
- targets: float32 [16384, 1024], P('dev', 'grp')
The draws below stay inside these ranges and needn't reach their ends.
All inputs are finite; a program needn't handle non-finite values.
Results may differ from the reference program's by a relative error of at most 0.0027.
Values may be sent and summed in bfloat16 or wider, within the bound.
No kernel may reach another device: no remote copies, remote signals or barrier semaphores. Data moves between devices by JAX's collectives and lax.ppermute only.
A program may use at most 64 MiB of HBM per device.

```python
import math
import jax
import jax.numpy as jnp
from jax import lax

D = 1024
ITERS = 4
NOISE = 16384
DATA = 16384


def draw_noise_draws(key, part):
    first_key = jax.random.fold_in(key, 0)
    values = jax.random.normal(first_key, (NOISE, D), jnp.float32)
    return jnp.clip(values, -12.0, 12.0).astype(jnp.bfloat16)


def steps_of(key, shape, cuts, low, largest):
    def one(dim, shards_of):
        draws = jax.random.uniform(jax.random.fold_in(jax.random.fold_in(key, 6), dim), (shards_of,), jnp.float32, low / len(cuts), largest / len(cuts))
        return jnp.repeat(jnp.exp(draws), shape[dim] // shards_of).reshape((-1,) + (1,) * (len(shape) - dim - 1))

    factor_of = one(*cuts[0])
    for cut in cuts[1:]:
        factor_of = factor_of * one(*cut)
    return factor_of


def scatter_about(stream_key, extent, scale, limit, shards=(), held_as=jnp.bfloat16):
    factor_of = steps_of(stream_key, extent, shards, -0.22, 0.18) if shards else 1.0
    result = jax.random.normal(stream_key, extent, jnp.float32) * scale * factor_of
    return jnp.minimum(jnp.maximum(result, -limit), limit).astype(held_as)


def setup_inputs(seed: int = 0) -> dict:
    streams_of = jax.random.split(jax.random.key(seed), 3)
    noise_draws = draw_noise_draws(jax.random.fold_in(streams_of[2], 71), 0)
    latents = scatter_about(streams_of[1], (DATA, D), 1.0, 6.0, ((0, 256),))
    return dict(noise_draws=noise_draws, latents=latents)


def reference(noise_draws, latents):
    epsilon = 1.0 / math.sqrt(D)
    noise_sq = lax.optimization_barrier(jnp.sum(jnp.square(noise_draws.astype(jnp.float32)), axis=1))
    latent_sq = lax.optimization_barrier(jnp.sum(jnp.square(latents.astype(jnp.float32)), axis=1))
    cross_term = jnp.dot(noise_draws, latents.T, preferred_element_type=jnp.float32)
    cost_full = (noise_sq[:, None] + latent_sq[None, :] - 2.0 * cross_term) / D
    log_rows = -math.log(NOISE)
    log_cols = -math.log(DATA)
    column_dual = jnp.zeros((DATA,), jnp.float32)
    for sweep in range(ITERS):
        row_total = jax.nn.logsumexp((column_dual[None, :] - cost_full) / epsilon, axis=1)
        row_dual = epsilon * log_rows - epsilon * row_total
        column_total = jax.nn.logsumexp((row_dual[:, None] - cost_full) / epsilon, axis=0)
        column_dual = epsilon * log_cols - epsilon * column_total
    logits = (column_dual[None, :] - cost_full) / epsilon
    norm_total = jax.nn.logsumexp(logits, axis=1)
    weights = jnp.exp(logits - norm_total[:, None]).astype(jnp.bfloat16)
    return jnp.dot(weights, latents, preferred_element_type=jnp.float32)
```

```python
import functools
import math

import jax
import jax.numpy as jnp
from jax import lax
from jax.experimental import pallas as pl
from jax.experimental.pallas import tpu as pltpu
from jax.sharding import Mesh
from jax.sharding import PartitionSpec as P


ITERS = 4
AXES = ("y_lo", "x", "y_hi", "z", "core")
SIZES = (2, 4, 2, 8, 2)
ROW = ("y_lo", "x", "core")
COL = ("y_hi", "z")
OWNERS = ("x", "y_lo")
BLOCKS = (0, 4, 1, 5, 2, 6, 3, 7)
FEATURES = 1024
ROWS = 1024
COLS = 1024
SAMPLES = 16384
STEP = 128
TINY = 2.0**-90
LARGE = 2.0**100
SHIFT = math.log2(SAMPLES)
SCALE = math.sqrt(FEATURES) * math.log2(math.e)
VMEM = pl.BlockSpec(memory_space=pltpu.VMEM)
SMEM = pl.BlockSpec(memory_space=pltpu.SMEM)
F32 = jnp.float32
BF16 = jnp.bfloat16


def call(kernel, out, scratch=(), flops=0, scalars=0, arrays=0, limit=8, aliases=None, kept=()):
    return pl.pallas_call(
        kernel,
        out_shape=out,
        in_specs=[
            pl.BlockSpec(memory_space=pl.ANY) if k in kept else SMEM if k < scalars else VMEM
            for k in range(scalars + arrays)
        ],
        out_specs=jax.tree.map(lambda _: VMEM, out),
        scratch_shapes=list(scratch),
        input_output_aliases=aliases or {},
        compiler_params=pltpu.CompilerParams(vmem_limit_bytes=limit << 20),
        cost_estimate=pl.CostEstimate(flops=flops, bytes_accessed=4 << 20, transcendentals=1 << 20),
    )


def diagonal():
    return lax.broadcasted_iota(jnp.int32, (128, 128), 0) == lax.broadcasted_iota(
        jnp.int32, (128, 128), 1
    )


def to_lanes(column, eye):
    parts = []
    for k in range(column.shape[0] // 128):
        spread = jnp.broadcast_to(column[k * 128 : (k + 1) * 128], (128, 128))
        parts.append(jnp.sum(jnp.where(eye, spread, 0.0), axis=0, keepdims=True))
    return jnp.concatenate(parts, axis=0)


def to_sublanes(line):
    return jnp.broadcast_to(line, (128, 128)).T


def joined_lse(parts):
    top = jnp.max(parts, axis=0)
    return top + jnp.log2(jnp.sum(jnp.exp2(parts - top[None]), axis=0))


def row_part(tile_ref, dual, out_ref, lse_ref):
    lines = [jnp.broadcast_to(dual[k : k + 1], (8, 128)) for k in range(8)]
    step = 64

    @pl.loop(0, ROWS // step)
    def _(at):
        rows = pl.ds(pl.multiple_of(at * step, step), step)
        logits = [
            tile_ref[rows, k * 128 : (k + 1) * 128] + jnp.tile(lines[k], (step // 8, 1))
            for k in range(8)
        ]
        top = logits[0]
        for part in logits[1:]:
            top = jnp.maximum(top, part)
        top = jnp.max(top, axis=1, keepdims=True)
        mass = jnp.exp2(logits[0] - top)
        for part in logits[1:]:
            mass = mass + jnp.exp2(part - top)
        mass = jnp.sum(mass, axis=1, keepdims=True)
        lse_ref[rows, :] = jnp.broadcast_to(top + jnp.log2(mass), (step, 128))

    out_ref[...] = jnp.broadcast_to(to_lanes(lse_ref[...], diagonal())[None], out_ref.shape)


def column_part(tile_ref, dual, out_ref, dual_ref):
    for k in range(8):
        dual_ref[k * 128 : (k + 1) * 128, :] = to_sublanes(dual[k : k + 1])
    step = 32

    def shifted(at, k):
        rows = pl.ds(pl.multiple_of(at * step, step), step)
        return tile_ref[rows, k * 128 : (k + 1) * 128] + dual_ref[rows, :]

    def peak(at, tops):
        return tuple(
            jnp.maximum(top, jnp.max(shifted(at, k).reshape(step // 8, 8, 128), axis=0))
            for k, top in enumerate(tops)
        )

    low = jnp.full((8, 128), -jnp.inf, F32)
    tops = lax.fori_loop(0, ROWS // step, peak, (low,) * 8)
    tops = [jnp.max(top, axis=0, keepdims=True) for top in tops]
    wide = [jnp.broadcast_to(top, (step, 128)) for top in tops]

    def add(at, sums):
        return tuple(
            total + jnp.sum(jnp.exp2(shifted(at, k) - wide[k]).reshape(step // 8, 8, 128), axis=0)
            for k, total in enumerate(sums)
        )

    sums = lax.fori_loop(0, ROWS // step, add, (jnp.zeros((8, 128), F32),) * 8)
    lse = jnp.concatenate(
        [
            top + jnp.log2(jnp.sum(total, axis=0, keepdims=True))
            for top, total in zip(tops, sums)
        ],
        axis=0,
    )
    out_ref[...] = jnp.broadcast_to(lse[None], out_ref.shape)


def lane_sums(wide):
    ones = jnp.ones((8, 128), BF16)
    rest, total = wide, 0.0
    for _ in range(3):
        piece = rest.astype(BF16)
        rest = rest - piece.astype(F32)
        total = total + lax.dot_general(
            ones, piece, (((1,), (1,)), ((), ())), preferred_element_type=F32
        )
    return jnp.concatenate(
        [total[0:1, k * 128 : (k + 1) * 128] for k in range(wide.shape[0] // 128)], axis=0
    )


def row_kernel(terms_ref, tile_ref, parts_ref, base_ref, out_ref, sums_ref):
    dual = -SHIFT - joined_lse(parts_ref[...])
    top = jnp.max(dual)
    factor = jnp.exp2(dual - top)
    lines = [jnp.broadcast_to(factor[k : k + 1], (8, 128)) for k in range(8)]

    @pl.loop(0, ROWS // STEP)
    def _(at):
        for q in range(STEP // 8):
            rows = pl.ds(pl.multiple_of(at * STEP + q * 8, 8), 8)
            mass = None
            for k in range(8):
                term = terms_ref[rows, k * 128 : (k + 1) * 128] * lines[k]
                mass = term if mass is None else mass + term
            sums_ref[rows, :] = mass

    total = lane_sums(sums_ref[...])
    lse = (top - SHIFT) - base_ref[...] + jnp.log2(total)
    out_ref[...] = jnp.broadcast_to(lse[None], out_ref.shape)

    @pl.when(jnp.min(total) < TINY)
    def _():
        row_part(tile_ref, dual, out_ref, sums_ref)


def column_total(sums):
    return jnp.concatenate([jnp.sum(part, axis=0, keepdims=True) for part in sums], axis=0)


def column_kernel(terms_ref, tile_ref, parts_ref, base_ref, out_ref, wide_ref):
    dual = -SHIFT - joined_lse(parts_ref[...])
    change = dual - base_ref[...]
    top = jnp.max(change)
    factor = jnp.exp2(change - top)
    for k in range(8):
        wide_ref[k * 128 : (k + 1) * 128, :] = to_sublanes(factor[k : k + 1])

    def add(at, sums):
        sums = list(sums)
        for q in range(STEP // 8):
            rows = pl.ds(pl.multiple_of(at * STEP + q * 8, 8), 8)
            share = wide_ref[rows, :]
            for k in range(8):
                sums[k] = sums[k] + terms_ref[rows, k * 128 : (k + 1) * 128] * share
        return tuple(sums)

    sums = lax.fori_loop(0, ROWS // STEP, add, (jnp.zeros((8, 128), F32),) * 8)
    total = column_total(sums)
    out_ref[...] = jnp.broadcast_to(((top - SHIFT) + jnp.log2(total))[None], out_ref.shape)

    @pl.when(jnp.min(total) < TINY)
    def _():
        column_part(tile_ref, dual, out_ref, wide_ref)


def first_column_kernel(tile_ref, parts_ref, out_ref, dual_ref, terms_ref, wide_ref):
    dual = -SHIFT - joined_lse(parts_ref[...])
    dual_ref[...] = dual
    for k in range(8):
        wide_ref[k * 128 : (k + 1) * 128, :] = to_sublanes(dual[k : k + 1] + SHIFT)

    def add(at, sums):
        sums = list(sums)
        for q in range(STEP // 8):
            rows = pl.ds(pl.multiple_of(at * STEP + q * 8, 8), 8)
            shift = wide_ref[rows, :]
            for k in range(8):
                here = slice(k * 128, (k + 1) * 128)
                term = jnp.exp2(tile_ref[rows, here] + shift)
                terms_ref[rows, here] = term
                sums[k] = sums[k] + term
        return tuple(sums)

    sums = lax.fori_loop(0, ROWS // STEP, add, (jnp.zeros((8, 128), F32),) * 8)
    total = column_total(sums)
    out_ref[...] = jnp.broadcast_to((jnp.log2(total) - SHIFT)[None], out_ref.shape)

    @pl.when(jnp.min(total) < TINY)
    def _():
        column_part(tile_ref, dual, out_ref, wide_ref)


def noise_kernel(place_ref, parts_ref, rows_ref):
    for k in range(4):
        for other in range(2):
            at = jnp.bitwise_xor(place_ref[0], other) * 4 + k
            rows_ref[:, pl.ds(pl.multiple_of(at * 128, 128), 128)] = parts_ref[k, other]


def spread_kernel(noise_ref, other_ref, out_ref, sems):
    copies = [
        pltpu.make_async_copy(ref, out_ref.at[k, j], sems.at[k, j])
        for j, ref in enumerate((noise_ref, other_ref))
        for k in range(4)
    ]
    for copy in copies:
        copy.start()
    for copy in copies:
        copy.wait()


def pack_kernel(*refs):
    for k, ref in enumerate(refs[:-1]):
        refs[-1][k * 64 : (k + 1) * 64, :] = ref[...]


def squares(ref, rows):
    total = None
    for k in range(8):
        wide = ref[rows, k * 128 : (k + 1) * 128].astype(F32)
        total = wide * wide if total is None else total + wide * wide
    return jnp.sum(total, axis=1, keepdims=True)


def costs(noise, starts, block_ref, tile_ref, squares_ref, base, use):
    eye = diagonal()

    @pl.loop(0, 2)
    def _(at):
        cols = pl.ds(pl.multiple_of(base + at * 256, 256), 256)
        latent_sq = squares(block_ref, cols)
        for start, ref in zip(starts, noise):
            cross = lax.dot_general(
                ref[...], block_ref[cols, :], (((1,), (1,)), ((), ())), preferred_element_type=F32
            )
            rows, pair = pl.ds(start, 512), []
            for k in range(2):
                spread = jnp.broadcast_to(latent_sq[k * 128 : (k + 1) * 128], (128, 128))
                line = jnp.sum(jnp.where(eye, spread, 0.0), axis=0, keepdims=True)
                line = jnp.broadcast_to(line, (512, 128))
                cost = squares_ref[rows, :] + line - 2.0 * cross[:, k * 128 : (k + 1) * 128]
                cost = cost * (-SCALE / FEATURES)
                tile_ref[rows, pl.ds(pl.multiple_of(base + at * 256 + k * 128, 128), 128)] = cost
                pair.append(cost)
            use(at, rows, pair)


def halves(core):
    return [pl.multiple_of(jnp.bitwise_xor(core, half) * 512, 512) for half in range(2)]


def placed(packs, block_ref, group, z, orders):
    for pack, backs in zip(packs, orders):
        for k, back in enumerate(backs):
            at = group * 8 + jnp.bitwise_and(z - back + 8, 7)
            rows = pl.ds(pl.multiple_of(at * 64, 64), 64)
            block_ref[rows, :] = pack[k * 64 : (k + 1) * 64, :]


def first_masses(tile_ref, base, top_ref, sums_ref):
    @pl.loop(0, ROWS // STEP)
    def _(at):
        for q in range(STEP // 8):
            rows = pl.ds(pl.multiple_of(at * STEP + q * 8, 8), 8)
            top = jnp.broadcast_to(jnp.max(top_ref[rows, :], axis=1, keepdims=True), (8, 128))
            top_ref[rows, :] = top
            mass = None
            for k in range(4):
                cols = pl.ds(pl.multiple_of(base + k * 128, 128), 128)
                term = jnp.exp2(tile_ref[rows, cols] - top)
                mass = term if mass is None else mass + term
            sums_ref[rows, :] = mass


def near_kernel(place_ref, *refs):
    noise, own_ref, near = refs[:2], refs[2], refs[3:7]
    block_ref, tile_ref, squares_ref, top_ref, sums_ref, line_ref, sem = refs[7:]
    y_hi, z, core = (place_ref[k] for k in range(2, 5))
    at = pl.multiple_of((y_hi * 8 + z) * 64, 64)
    fetch = pltpu.make_async_copy(own_ref, block_ref.at[pl.ds(at, 64), :], sem)
    fetch.start()
    placed(near, block_ref, y_hi, z, PACKS[1:])
    starts = halves(core)
    for start, ref in zip(starts, noise):
        for k in range(4):
            squares_ref[pl.ds(start + k * 128, 128), :] = jnp.broadcast_to(
                squares(ref, slice(k * 128, (k + 1) * 128)), (128, 128)
            )
    fetch.wait()
    base = pl.multiple_of(y_hi * 512, 512)

    def use(at, rows, pair):
        top = jnp.maximum(*pair)
        top_ref[rows, :] = jnp.maximum(jnp.where(at == 0, top, top_ref[rows, :]), top)

    costs(noise, starts, block_ref, tile_ref, squares_ref, base, use)
    first_masses(tile_ref, base, top_ref, sums_ref)
    line_ref[...] = to_lanes(top_ref[...], diagonal())


def far_kernel(place_ref, *refs):
    noise, far = refs[:2], refs[2:7]
    squares_ref, top_ref, near_sums_ref, line_ref, _, _ = refs[7:13]
    block_ref, tile_ref, out_ref, sums_ref = refs[13:]
    y_hi, z, core = (place_ref[k] for k in range(2, 5))
    placed(far, block_ref, 1 - y_hi, z, PACKS)
    base = pl.multiple_of((1 - y_hi) * 512, 512)
    sums_ref[...] = near_sums_ref[...]

    def use(at, rows, pair):
        top = top_ref[rows, :]
        sums_ref[rows, :] = sums_ref[rows, :] + (jnp.exp2(pair[0] - top) + jnp.exp2(pair[1] - top))

    costs(noise, halves(core), block_ref, tile_ref, squares_ref, base, use)
    largest = jnp.max(sums_ref[...])
    lse = line_ref[...] + jnp.log2(lane_sums(sums_ref[...]))
    out_ref[...] = jnp.broadcast_to(lse[None], out_ref.shape)

    @pl.when(jnp.logical_not(largest < LARGE))
    def _():
        row_part(tile_ref, jnp.zeros((8, 128), F32), out_ref, sums_ref)


def last_kernel(
    mine, skip, core_ref, terms_ref, tile_ref, parts_ref, base_ref, block_ref,
    out_ref, limit_ref, mass_ref, wide_ref, sums_ref, weights_ref,
):
    count = out_ref.shape[0]
    half = core_ref[0] if mine else 1 - core_ref[0]
    first = pl.multiple_of(half * 512 + skip, 128)
    dual = -SHIFT - joined_lse(parts_ref[...])
    top = jnp.max(dual)
    factor = jnp.exp2(dual - top)
    lines = slice(skip // 128, (skip + count) // 128)
    base = jnp.where(half == 0, base_ref[0:4], base_ref[4:8])[lines]

    def keep(start, values):
        mass = None
        for k, term in enumerate(values):
            mass = term if mass is None else mass + term
            weights_ref[pl.ds(start, 16), k * 128 : (k + 1) * 128] = term.astype(BF16)
        sums_ref[pl.ds(start, 16), :] = mass

    shares = [jnp.broadcast_to(factor[k : k + 1], (16, 128)) for k in range(8)]

    @pl.loop(0, count // 128)
    def _(at):
        for q in range(8):
            start = pl.multiple_of(at * 128 + q * 16, 16)
            rows = pl.ds(pl.multiple_of(first + start, 16), 16)
            keep(start, [terms_ref[rows, k * 128 : (k + 1) * 128] * shares[k] for k in range(8)])

    limit_ref[...] = (top - SHIFT) - base
    mass_ref[...] = lane_sums(sums_ref[...])

    @pl.when(jnp.min(mass_ref[...]) < TINY)
    def _():
        duals = [jnp.broadcast_to(dual[k : k + 1], (16, 128)) for k in range(8)]

        @pl.loop(0, count // 16)
        def _(at):
            start = pl.multiple_of(at * 16, 16)
            rows = pl.ds(pl.multiple_of(first + start, 16), 16)
            logits = [tile_ref[rows, k * 128 : (k + 1) * 128] + duals[k] for k in range(8)]
            peak = logits[0]
            for part in logits[1:]:
                peak = jnp.maximum(peak, part)
            peak = jnp.broadcast_to(jnp.max(peak, axis=1, keepdims=True), (16, 128))
            wide_ref[pl.ds(start, 16), :] = peak
            keep(start, [jnp.exp2(part - peak) for part in logits])

        limit_ref[...] = to_lanes(wide_ref[...], diagonal())
        mass_ref[...] = lane_sums(sums_ref[...])

    @pl.loop(0, 4)
    def _(at):
        here = pl.ds(pl.multiple_of(at * 256, 256), 256)
        out_ref[:, here] = jnp.dot(
            weights_ref[...], block_ref[:, here], preferred_element_type=F32
        ).astype(out_ref.dtype)


def pieces_of(value):
    pieces = []
    for _ in range(3):
        pieces.append(value.astype(BF16))
        value = value - pieces[-1].astype(F32)
    return pieces


def cores_kernel(
    skip, mine_ref, limit_ref, mass_ref, other_ref, other_limit_ref, other_mass_ref, out_ref
):
    count = mine_ref.shape[0]
    lines = slice(skip // 128, (skip + count) // 128)
    other_limit, other_mass = other_limit_ref[...][lines], other_mass_ref[...][lines]
    limit = jnp.maximum(limit_ref[...], other_limit)
    a, b = jnp.exp2(limit_ref[...] - limit), jnp.exp2(other_limit - limit)
    mass = a * mass_ref[...] + b * other_mass
    for k in range(count // 128):
        wide_a, wide_b = to_sublanes(a[k : k + 1]), to_sublanes(b[k : k + 1])
        rows = slice(k * 128, (k + 1) * 128)
        other_rows = slice(skip + k * 128, skip + (k + 1) * 128)
        for g, block in enumerate(BLOCKS):
            here = slice(block * 128, (block + 1) * 128)
            out_ref[g, rows, :] = (
                wide_a * mine_ref[rows, here] + wide_b * other_ref[other_rows, here].astype(F32)
            ).astype(BF16)
    pieces = pieces_of(limit) + pieces_of(mass)
    pieces = jnp.concatenate(pieces + [jnp.zeros_like(pieces[0])] * 2, axis=0)
    for g in range(8):
        out_ref[g, count:, :] = pieces


def groups_kernel(*refs):
    out_ref, start = refs[-1], 0
    for parts_ref in refs[:-1]:
        count = parts_ref.shape[1] // 136 * 128
        n = count // 128
        pieces = parts_ref[:, count:, :].astype(F32)
        limit = pieces[:, 0:n] + pieces[:, n : 2 * n] + pieces[:, 2 * n : 3 * n]
        mass = pieces[:, 3 * n : 4 * n] + pieces[:, 4 * n : 5 * n] + pieces[:, 5 * n : 6 * n]
        share = jnp.exp2(limit - jnp.max(limit, axis=0)[None])
        share = share / jnp.sum(share * mass, axis=0)[None]
        for k in range(n):
            total = jnp.zeros((128, 128), F32)
            for g in range(8):
                total = total + to_sublanes(share[g, k : k + 1]) * parts_ref[
                    g, k * 128 : (k + 1) * 128, :
                ].astype(F32)
            out_ref[start + k * 128 : start + (k + 1) * 128, :] = total
        start += count


def moved(array, axis, step):
    size = lax.axis_size(axis)
    return lax.ppermute(array, axis, [(k, (k + step) % size) for k in range(size)])


def exchanged(parts, axes):
    return lax.all_to_all(parts, axes, 0, 0, tiled=True)


def local(noise_draws, latents):
    place = jnp.stack([lax.axis_index(axis) for axis in AXES]).astype(jnp.int32)
    part = jax.ShapeDtypeStruct((16, 8, 128), F32)
    line = jax.ShapeDtypeStruct((8, 128), F32)
    wide = pltpu.VMEM((ROWS, 128), F32)

    block_out = jax.ShapeDtypeStruct((COLS, FEATURES), BF16)
    tile_out = jax.ShapeDtypeStruct((ROWS, COLS), F32)
    wide_out = jax.ShapeDtypeStruct((ROWS, 128), F32)

    near, far = [latents] + [None] * 7, []
    near[1] = moved(latents, "z", 1)
    near[7] = moved(latents, "z", -1)
    near[2] = moved(near[1], "z", 1)
    near[6] = moved(near[7], "z", -1)
    near[3] = moved(near[2], "z", 1)
    near[5] = moved(near[6], "z", -1)
    near[4] = moved(near[2], "z", 2)
    packs = []
    for backs in PACKS:
        if len(backs) == 1:
            packs.append(near[backs[0]])
            continue
        packs.append(
            call(
                pack_kernel,
                jax.ShapeDtypeStruct((64 * len(backs), FEATURES), BF16),
                arrays=len(backs),
                limit=2,
            )(*(near[back] for back in backs))
        )
    far = [moved(pack, "y_hi", 1) for pack in packs]
    noise_pair = moved(noise_draws, "y_lo", 1)
    spread = pl.pallas_call(
        spread_kernel,
        out_shape=jax.ShapeDtypeStruct((4, 2, *noise_draws.shape), BF16),
        in_specs=[VMEM, VMEM],
        out_specs=pl.BlockSpec(memory_space=pl.ANY),
        scratch_shapes=[pltpu.SemaphoreType.DMA((4, 2))],
        name="spread",
        compiler_params=pltpu.CompilerParams(vmem_limit_bytes=2 << 20),
    )(noise_draws, noise_pair)
    features = exchanged(spread, "x")
    rows = call(
        noise_kernel, jax.ShapeDtypeStruct((512, FEATURES), BF16), scalars=1, arrays=1, limit=4
    )(place, features)
    other_rows = moved(rows, "core", 1)
    block, tile, squared, top, masses, peaks = call(
        near_kernel,
        (block_out, tile_out, wide_out, wide_out, wide_out, line),
        [pltpu.SemaphoreType.DMA],
        flops=1 << 30,
        scalars=1,
        arrays=7,
        kept=(3,),
    )(place, rows, other_rows, *packs)
    block, tile, parts = call(
        far_kernel, (block_out, tile_out, part), [wide], 1 << 30, 1, 13, aliases={12: 0, 13: 1}
    )(place, rows, other_rows, *far, squared, top, masses, peaks, block, tile)
    for sweep in range(ITERS):
        if sweep:
            parts = call(row_kernel, part, [wide], arrays=4)(terms, tile, parts, base)
        parts = exchanged(parts, ROW)
        if sweep:
            parts = call(column_kernel, part, [wide], arrays=4)(terms, tile, parts, base)
        else:
            parts, base, terms = call(
                first_column_kernel, (part, line, tile_out), [wide], arrays=2
            )(tile, parts)
        parts = exchanged(parts, COL)
    core = place[4:5]

    def last(mine, skip, count, dtype):
        lines = jax.ShapeDtypeStruct((count // 128, 128), F32)
        spare = pltpu.VMEM((count, 128), F32)
        return call(
            functools.partial(last_kernel, mine, skip),
            (jax.ShapeDtypeStruct((count, FEATURES), dtype), lines, lines),
            [spare, spare, pltpu.VMEM((count, COLS), BF16)],
            count << 21,
            1,
            5,
        )(core, terms, tile, parts, base, block)

    away = last(False, 0, 512, BF16)
    other = [moved(value, "core", 1) for value in away]
    messages, skip = [], 0
    for count in OWN:
        own = last(True, skip, count, F32)
        message = call(
            functools.partial(cores_kernel, skip),
            jax.ShapeDtypeStruct((8, count // 128 * 136, 128), BF16),
            arrays=6,
        )(*own, *other)
        messages.append(exchanged(message, OWNERS))
        skip += count
    return call(
        groups_kernel, jax.ShapeDtypeStruct((512, 128), F32), arrays=len(messages)
    )(*messages)


OWN = (512,)
PACKS = ((0,), (1, 7), (2, 6), (3, 5), (4,))


def solution(mesh):
    torus = Mesh(mesh.devices.reshape(SIZES), AXES)
    rows = P(("y_hi", "z", "core"), ("y_lo", "x"))
    return jax.shard_map(
        local, mesh=torus, in_specs=(rows, P(AXES, None)), out_specs=rows, check_vma=False
    )
```

```python
import functools
import math

import jax
import jax.numpy as jnp
from jax import lax
from jax.experimental import pallas as pl
from jax.experimental.pallas import tpu as pltpu
from jax.sharding import Mesh
from jax.sharding import PartitionSpec as P


ITERS = 4
AXES = ("y_lo", "x", "y_hi", "z", "core")
SIZES = (2, 4, 2, 8, 2)
ROW = ("y_lo", "x", "core")
COL = ("y_hi", "z")
OWNERS = ("x", "y_lo")
BLOCKS = (0, 4, 1, 5, 2, 6, 3, 7)
FEATURES = 1024
ROWS = 1024
COLS = 1024
SAMPLES = 16384
STEP = 128
TINY = 2.0**-90
LARGE = 2.0**100
SHIFT = math.log2(SAMPLES)
SCALE = math.sqrt(FEATURES) * math.log2(math.e)
VMEM = pl.BlockSpec(memory_space=pltpu.VMEM)
SMEM = pl.BlockSpec(memory_space=pltpu.SMEM)
F32 = jnp.float32
BF16 = jnp.bfloat16


def call(kernel, out, scratch=(), flops=0, scalars=0, arrays=0, limit=8, aliases=None, kept=()):
    return pl.pallas_call(
        kernel,
        out_shape=out,
        in_specs=[
            pl.BlockSpec(memory_space=pl.ANY) if k in kept else SMEM if k < scalars else VMEM
            for k in range(scalars + arrays)
        ],
        out_specs=jax.tree.map(lambda _: VMEM, out),
        scratch_shapes=list(scratch),
        input_output_aliases=aliases or {},
        compiler_params=pltpu.CompilerParams(vmem_limit_bytes=limit << 20),
        cost_estimate=pl.CostEstimate(flops=flops, bytes_accessed=4 << 20, transcendentals=1 << 20),
    )


def diagonal():
    return lax.broadcasted_iota(jnp.int32, (128, 128), 0) == lax.broadcasted_iota(
        jnp.int32, (128, 128), 1
    )


def to_lanes(column, eye):
    parts = []
    for k in range(column.shape[0] // 128):
        spread = jnp.broadcast_to(column[k * 128 : (k + 1) * 128], (128, 128))
        parts.append(jnp.sum(jnp.where(eye, spread, 0.0), axis=0, keepdims=True))
    return jnp.concatenate(parts, axis=0)


def to_sublanes(line):
    return jnp.broadcast_to(line, (128, 128)).T


def joined_lse(parts):
    top = jnp.max(parts, axis=0)
    return top + jnp.log2(jnp.sum(jnp.exp2(parts - top[None]), axis=0))


def row_part(tile_ref, dual, out_ref, lse_ref):
    lines = [jnp.broadcast_to(dual[k : k + 1], (8, 128)) for k in range(8)]
    step = 64

    @pl.loop(0, ROWS // step)
    def _(at):
        rows = pl.ds(pl.multiple_of(at * step, step), step)
        logits = [
            tile_ref[rows, k * 128 : (k + 1) * 128] + jnp.tile(lines[k], (step // 8, 1))
            for k in range(8)
        ]
        top = logits[0]
        for part in logits[1:]:
            top = jnp.maximum(top, part)
        top = jnp.max(top, axis=1, keepdims=True)
        mass = jnp.exp2(logits[0] - top)
        for part in logits[1:]:
            mass = mass + jnp.exp2(part - top)
        mass = jnp.sum(mass, axis=1, keepdims=True)
        lse_ref[rows, :] = jnp.broadcast_to(top + jnp.log2(mass), (step, 128))

    out_ref[...] = jnp.broadcast_to(to_lanes(lse_ref[...], diagonal())[None], out_ref.shape)


def column_part(tile_ref, dual, out_ref, dual_ref):
    for k in range(8):
        dual_ref[k * 128 : (k + 1) * 128, :] = to_sublanes(dual[k : k + 1])
    step = 32

    def shifted(at, k):
        rows = pl.ds(pl.multiple_of(at * step, step), step)
        return tile_ref[rows, k * 128 : (k + 1) * 128] + dual_ref[rows, :]

    def peak(at, tops):
        return tuple(
            jnp.maximum(top, jnp.max(shifted(at, k).reshape(step // 8, 8, 128), axis=0))
            for k, top in enumerate(tops)
        )

    low = jnp.full((8, 128), -jnp.inf, F32)
    tops = lax.fori_loop(0, ROWS // step, peak, (low,) * 8)
    tops = [jnp.max(top, axis=0, keepdims=True) for top in tops]
    wide = [jnp.broadcast_to(top, (step, 128)) for top in tops]

    def add(at, sums):
        return tuple(
            total + jnp.sum(jnp.exp2(shifted(at, k) - wide[k]).reshape(step // 8, 8, 128), axis=0)
            for k, total in enumerate(sums)
        )

    sums = lax.fori_loop(0, ROWS // step, add, (jnp.zeros((8, 128), F32),) * 8)
    lse = jnp.concatenate(
        [
            top + jnp.log2(jnp.sum(total, axis=0, keepdims=True))
            for top, total in zip(tops, sums)
        ],
        axis=0,
    )
    out_ref[...] = jnp.broadcast_to(lse[None], out_ref.shape)


def lane_sums(wide):
    ones = jnp.ones((8, 128), BF16)
    rest, total = wide, 0.0
    for _ in range(3):
        piece = rest.astype(BF16)
        rest = rest - piece.astype(F32)
        total = total + lax.dot_general(
            ones, piece, (((1,), (1,)), ((), ())), preferred_element_type=F32
        )
    return jnp.concatenate(
        [total[0:1, k * 128 : (k + 1) * 128] for k in range(wide.shape[0] // 128)], axis=0
    )


def row_kernel(terms_ref, tile_ref, parts_ref, base_ref, out_ref, sums_ref):
    dual = -SHIFT - joined_lse(parts_ref[...])
    top = jnp.max(dual)
    factor = jnp.exp2(dual - top)
    lines = [jnp.broadcast_to(factor[k : k + 1], (8, 128)) for k in range(8)]

    @pl.loop(0, ROWS // STEP)
    def _(at):
        for q in range(STEP // 8):
            rows = pl.ds(pl.multiple_of(at * STEP + q * 8, 8), 8)
            mass = None
            for k in range(8):
                term = terms_ref[rows, k * 128 : (k + 1) * 128] * lines[k]
                mass = term if mass is None else mass + term
            sums_ref[rows, :] = mass

    total = lane_sums(sums_ref[...])
    lse = (top - SHIFT) - base_ref[...] + jnp.log2(total)
    out_ref[...] = jnp.broadcast_to(lse[None], out_ref.shape)

    @pl.when(jnp.min(total) < TINY)
    def _():
        row_part(tile_ref, dual, out_ref, sums_ref)


def column_total(sums):
    return jnp.concatenate([jnp.sum(part, axis=0, keepdims=True) for part in sums], axis=0)


def column_kernel(terms_ref, tile_ref, parts_ref, base_ref, out_ref, wide_ref):
    dual = -SHIFT - joined_lse(parts_ref[...])
    change = dual - base_ref[...]
    top = jnp.max(change)
    factor = jnp.exp2(change - top)
    for k in range(8):
        wide_ref[k * 128 : (k + 1) * 128, :] = to_sublanes(factor[k : k + 1])

    def add(at, sums):
        sums = list(sums)
        for q in range(STEP // 8):
            rows = pl.ds(pl.multiple_of(at * STEP + q * 8, 8), 8)
            share = wide_ref[rows, :]
            for k in range(8):
                sums[k] = sums[k] + terms_ref[rows, k * 128 : (k + 1) * 128] * share
        return tuple(sums)

    sums = lax.fori_loop(0, ROWS // STEP, add, (jnp.zeros((8, 128), F32),) * 8)
    total = column_total(sums)
    out_ref[...] = jnp.broadcast_to(((top - SHIFT) + jnp.log2(total))[None], out_ref.shape)

    @pl.when(jnp.min(total) < TINY)
    def _():
        column_part(tile_ref, dual, out_ref, wide_ref)


def first_column_kernel(tile_ref, parts_ref, out_ref, dual_ref, terms_ref, wide_ref):
    dual = -SHIFT - joined_lse(parts_ref[...])
    dual_ref[...] = dual
    for k in range(8):
        wide_ref[k * 128 : (k + 1) * 128, :] = to_sublanes(dual[k : k + 1] + SHIFT)

    def add(at, sums):
        sums = list(sums)
        for q in range(STEP // 8):
            rows = pl.ds(pl.multiple_of(at * STEP + q * 8, 8), 8)
            shift = wide_ref[rows, :]
            for k in range(8):
                here = slice(k * 128, (k + 1) * 128)
                term = jnp.exp2(tile_ref[rows, here] + shift)
                terms_ref[rows, here] = term
                sums[k] = sums[k] + term
        return tuple(sums)

    sums = lax.fori_loop(0, ROWS // STEP, add, (jnp.zeros((8, 128), F32),) * 8)
    total = column_total(sums)
    out_ref[...] = jnp.broadcast_to((jnp.log2(total) - SHIFT)[None], out_ref.shape)

    @pl.when(jnp.min(total) < TINY)
    def _():
        column_part(tile_ref, dual, out_ref, wide_ref)


def noise_kernel(place_ref, parts_ref, rows_ref):
    for k in range(4):
        for other in range(2):
            at = jnp.bitwise_xor(place_ref[0], other) * 4 + k
            rows_ref[:, pl.ds(pl.multiple_of(at * 128, 128), 128)] = parts_ref[k, other]


def spread_kernel(noise_ref, other_ref, out_ref, sems):
    copies = [
        pltpu.make_async_copy(ref, out_ref.at[k, j], sems.at[k, j])
        for j, ref in enumerate((noise_ref, other_ref))
        for k in range(4)
    ]
    for copy in copies:
        copy.start()
    for copy in copies:
        copy.wait()


def pack_kernel(*refs):
    for k, ref in enumerate(refs[:-1]):
        refs[-1][k * 64 : (k + 1) * 64, :] = ref[...]


def squares(ref, rows):
    total = None
    for k in range(8):
        wide = ref[rows, k * 128 : (k + 1) * 128].astype(F32)
        total = wide * wide if total is None else total + wide * wide
    return jnp.sum(total, axis=1, keepdims=True)


def costs(noise, starts, block_ref, tile_ref, squares_ref, base, use):
    eye = diagonal()

    @pl.loop(0, 2)
    def _(at):
        cols = pl.ds(pl.multiple_of(base + at * 256, 256), 256)
        latent_sq = squares(block_ref, cols)
        for start, ref in zip(starts, noise):
            cross = lax.dot_general(
                ref[...], block_ref[cols, :], (((1,), (1,)), ((), ())), preferred_element_type=F32
            )
            rows, pair = pl.ds(start, 512), []
            for k in range(2):
                spread = jnp.broadcast_to(latent_sq[k * 128 : (k + 1) * 128], (128, 128))
                line = jnp.sum(jnp.where(eye, spread, 0.0), axis=0, keepdims=True)
                line = jnp.broadcast_to(line, (512, 128))
                cost = squares_ref[rows, :] + line - 2.0 * cross[:, k * 128 : (k + 1) * 128]
                cost = cost * (-SCALE / FEATURES)
                tile_ref[rows, pl.ds(pl.multiple_of(base + at * 256 + k * 128, 128), 128)] = cost
                pair.append(cost)
            use(at, rows, pair)


def halves(core):
    return [pl.multiple_of(jnp.bitwise_xor(core, half) * 512, 512) for half in range(2)]


def placed(packs, block_ref, group, z, orders):
    for pack, backs in zip(packs, orders):
        for k, back in enumerate(backs):
            at = group * 8 + jnp.bitwise_and(z - back + 8, 7)
            rows = pl.ds(pl.multiple_of(at * 64, 64), 64)
            block_ref[rows, :] = pack[k * 64 : (k + 1) * 64, :]


def first_masses(tile_ref, base, top_ref, sums_ref):
    @pl.loop(0, ROWS // STEP)
    def _(at):
        for q in range(STEP // 8):
            rows = pl.ds(pl.multiple_of(at * STEP + q * 8, 8), 8)
            top = jnp.broadcast_to(jnp.max(top_ref[rows, :], axis=1, keepdims=True), (8, 128))
            top_ref[rows, :] = top
            mass = None
            for k in range(4):
                cols = pl.ds(pl.multiple_of(base + k * 128, 128), 128)
                term = jnp.exp2(tile_ref[rows, cols] - top)
                mass = term if mass is None else mass + term
            sums_ref[rows, :] = mass


def near_kernel(place_ref, *refs):
    noise, own_ref, near = refs[:2], refs[2], refs[3:8]
    block_ref, tile_ref, squares_ref, top_ref, sums_ref, line_ref, sem = refs[8:]
    y_hi, z, core = (place_ref[k] for k in range(2, 5))
    at = pl.multiple_of((y_hi * 8 + z) * 64, 64)
    fetch = pltpu.make_async_copy(own_ref, block_ref.at[pl.ds(at, 64), :], sem)
    fetch.start()
    placed(near, block_ref, y_hi, z, PACKS[1:])
    starts = halves(core)
    for start, ref in zip(starts, noise):
        for k in range(4):
            squares_ref[pl.ds(start + k * 128, 128), :] = jnp.broadcast_to(
                squares(ref, slice(k * 128, (k + 1) * 128)), (128, 128)
            )
    fetch.wait()
    base = pl.multiple_of(y_hi * 512, 512)

    def use(at, rows, pair):
        top = jnp.maximum(*pair)
        top_ref[rows, :] = jnp.maximum(jnp.where(at == 0, top, top_ref[rows, :]), top)

    costs(noise, starts, block_ref, tile_ref, squares_ref, base, use)
    first_masses(tile_ref, base, top_ref, sums_ref)
    line_ref[...] = to_lanes(top_ref[...], diagonal())


def far_kernel(place_ref, *refs):
    noise, far = refs[:2], refs[2:8]
    squares_ref, top_ref, near_sums_ref, line_ref, _, _ = refs[8:14]
    block_ref, tile_ref, out_ref, sums_ref = refs[14:]
    y_hi, z, core = (place_ref[k] for k in range(2, 5))
    placed(far, block_ref, 1 - y_hi, z, PACKS)
    base = pl.multiple_of((1 - y_hi) * 512, 512)
    sums_ref[...] = near_sums_ref[...]

    def use(at, rows, pair):
        top = top_ref[rows, :]
        sums_ref[rows, :] = sums_ref[rows, :] + (jnp.exp2(pair[0] - top) + jnp.exp2(pair[1] - top))

    costs(noise, halves(core), block_ref, tile_ref, squares_ref, base, use)
    largest = jnp.max(sums_ref[...])
    lse = line_ref[...] + jnp.log2(lane_sums(sums_ref[...]))
    out_ref[...] = jnp.broadcast_to(lse[None], out_ref.shape)

    @pl.when(jnp.logical_not(largest < LARGE))
    def _():
        row_part(tile_ref, jnp.zeros((8, 128), F32), out_ref, sums_ref)


def last_kernel(
    mine, skip, core_ref, terms_ref, tile_ref, parts_ref, base_ref, block_ref,
    out_ref, limit_ref, mass_ref, wide_ref, sums_ref, weights_ref,
):
    count = out_ref.shape[0]
    half = core_ref[0] if mine else 1 - core_ref[0]
    first = pl.multiple_of(half * 512 + skip, 128)
    dual = -SHIFT - joined_lse(parts_ref[...])
    top = jnp.max(dual)
    factor = jnp.exp2(dual - top)
    lines = slice(skip // 128, (skip + count) // 128)
    base = jnp.where(half == 0, base_ref[0:4], base_ref[4:8])[lines]

    def keep(start, values):
        mass = None
        for k, term in enumerate(values):
            mass = term if mass is None else mass + term
            weights_ref[pl.ds(start, 16), k * 128 : (k + 1) * 128] = term.astype(BF16)
        sums_ref[pl.ds(start, 16), :] = mass

    shares = [jnp.broadcast_to(factor[k : k + 1], (16, 128)) for k in range(8)]

    @pl.loop(0, count // 128)
    def _(at):
        for q in range(8):
            start = pl.multiple_of(at * 128 + q * 16, 16)
            rows = pl.ds(pl.multiple_of(first + start, 16), 16)
            keep(start, [terms_ref[rows, k * 128 : (k + 1) * 128] * shares[k] for k in range(8)])

    limit_ref[...] = (top - SHIFT) - base
    mass_ref[...] = lane_sums(sums_ref[...])

    @pl.when(jnp.min(mass_ref[...]) < TINY)
    def _():
        duals = [jnp.broadcast_to(dual[k : k + 1], (16, 128)) for k in range(8)]

        @pl.loop(0, count // 16)
        def _(at):
            start = pl.multiple_of(at * 16, 16)
            rows = pl.ds(pl.multiple_of(first + start, 16), 16)
            logits = [tile_ref[rows, k * 128 : (k + 1) * 128] + duals[k] for k in range(8)]
            peak = logits[0]
            for part in logits[1:]:
                peak = jnp.maximum(peak, part)
            peak = jnp.broadcast_to(jnp.max(peak, axis=1, keepdims=True), (16, 128))
            wide_ref[pl.ds(start, 16), :] = peak
            keep(start, [jnp.exp2(part - peak) for part in logits])

        limit_ref[...] = to_lanes(wide_ref[...], diagonal())
        mass_ref[...] = lane_sums(sums_ref[...])

    @pl.loop(0, 4)
    def _(at):
        here = pl.ds(pl.multiple_of(at * 256, 256), 256)
        out_ref[:, here] = jnp.dot(
            weights_ref[...], block_ref[:, here], preferred_element_type=F32
        ).astype(out_ref.dtype)


def pieces_of(value):
    pieces = []
    for _ in range(3):
        pieces.append(value.astype(BF16))
        value = value - pieces[-1].astype(F32)
    return pieces


def cores_kernel(
    skip, mine_ref, limit_ref, mass_ref, other_ref, other_limit_ref, other_mass_ref, out_ref
):
    count = mine_ref.shape[0]
    lines = slice(skip // 128, (skip + count) // 128)
    other_limit, other_mass = other_limit_ref[...][lines], other_mass_ref[...][lines]
    limit = jnp.maximum(limit_ref[...], other_limit)
    a, b = jnp.exp2(limit_ref[...] - limit), jnp.exp2(other_limit - limit)
    mass = a * mass_ref[...] + b * other_mass
    for k in range(count // 128):
        wide_a, wide_b = to_sublanes(a[k : k + 1]), to_sublanes(b[k : k + 1])
        rows = slice(k * 128, (k + 1) * 128)
        other_rows = slice(skip + k * 128, skip + (k + 1) * 128)
        for g, block in enumerate(BLOCKS):
            here = slice(block * 128, (block + 1) * 128)
            out_ref[g, rows, :] = (
                wide_a * mine_ref[rows, here] + wide_b * other_ref[other_rows, here].astype(F32)
            ).astype(BF16)
    pieces = pieces_of(limit) + pieces_of(mass)
    pieces = jnp.concatenate(pieces, axis=0)
    for g in range(8):
        out_ref[g, count:, :] = pieces


def groups_kernel(*refs):
    out_ref, start = refs[-1], 0
    for parts_ref in refs[:-1]:
        count = parts_ref.shape[1] // 134 * 128
        n = count // 128
        pieces = parts_ref[:, count:, :].astype(F32)
        limit = pieces[:, 0:n] + pieces[:, n : 2 * n] + pieces[:, 2 * n : 3 * n]
        mass = pieces[:, 3 * n : 4 * n] + pieces[:, 4 * n : 5 * n] + pieces[:, 5 * n : 6 * n]
        share = jnp.exp2(limit - jnp.max(limit, axis=0)[None])
        share = share / jnp.sum(share * mass, axis=0)[None]
        for k in range(n):
            total = jnp.zeros((128, 128), F32)
            for g in range(8):
                total = total + to_sublanes(share[g, k : k + 1]) * parts_ref[
                    g, k * 128 : (k + 1) * 128, :
                ].astype(F32)
            out_ref[start + k * 128 : start + (k + 1) * 128, :] = total
        start += count


def moved(array, axis, step):
    size = lax.axis_size(axis)
    return lax.ppermute(array, axis, [(k, (k + step) % size) for k in range(size)])


def exchanged(parts, axes):
    return lax.all_to_all(parts, axes, 0, 0, tiled=True)


def local(noise_draws, latents):
    place = jnp.stack([lax.axis_index(axis) for axis in AXES]).astype(jnp.int32)
    part = jax.ShapeDtypeStruct((16, 8, 128), F32)
    line = jax.ShapeDtypeStruct((8, 128), F32)
    wide = pltpu.VMEM((ROWS, 128), F32)

    block_out = jax.ShapeDtypeStruct((COLS, FEATURES), BF16)
    tile_out = jax.ShapeDtypeStruct((ROWS, COLS), F32)
    wide_out = jax.ShapeDtypeStruct((ROWS, 128), F32)

    near, far = [latents] + [None] * 7, []
    near[1] = moved(latents, "z", 1)
    near[7] = moved(latents, "z", -1)
    near[2] = moved(near[1], "z", 1)
    near[6] = moved(near[7], "z", -1)
    near[3] = moved(near[2], "z", 1)
    near[5] = moved(near[6], "z", -1)
    near[4] = moved(near[2], "z", 2)
    packs = []
    for backs in PACKS:
        if len(backs) == 1:
            packs.append(near[backs[0]])
            continue
        packs.append(
            call(
                pack_kernel,
                jax.ShapeDtypeStruct((64 * len(backs), FEATURES), BF16),
                arrays=len(backs),
                limit=2,
            )(*(near[back] for back in backs))
        )
    across = moved(latents, "y_hi", 1)
    far = [across, moved(across, "z", 1), moved(across, "z", -1)]
    far += [moved(packs[k], "y_hi", 1) for k in range(3, len(packs))]
    noise_pair = moved(noise_draws, "y_lo", 1)
    spread = pl.pallas_call(
        spread_kernel,
        out_shape=jax.ShapeDtypeStruct((4, 2, *noise_draws.shape), BF16),
        in_specs=[VMEM, VMEM],
        out_specs=pl.BlockSpec(memory_space=pl.ANY),
        scratch_shapes=[pltpu.SemaphoreType.DMA((4, 2))],
        name="spread",
        compiler_params=pltpu.CompilerParams(vmem_limit_bytes=2 << 20),
    )(noise_draws, noise_pair)
    features = exchanged(spread, "x")
    rows = call(
        noise_kernel, jax.ShapeDtypeStruct((512, FEATURES), BF16), scalars=1, arrays=1, limit=4
    )(place, features)
    other_rows = moved(rows, "core", 1)
    block, tile, squared, top, masses, peaks = call(
        near_kernel,
        (block_out, tile_out, wide_out, wide_out, wide_out, line),
        [pltpu.SemaphoreType.DMA],
        flops=1 << 30,
        scalars=1,
        arrays=8,
        kept=(3,),
    )(place, rows, other_rows, *packs)
    block, tile, parts = call(
        far_kernel, (block_out, tile_out, part), [wide], 1 << 30, 1, 14, aliases={13: 0, 14: 1}
    )(place, rows, other_rows, *far, squared, top, masses, peaks, block, tile)
    for sweep in range(ITERS):
        if sweep:
            parts = call(row_kernel, part, [wide], arrays=4)(terms, tile, parts, base)
        parts = exchanged(parts, ROW)
        if sweep:
            parts = call(column_kernel, part, [wide], arrays=4)(terms, tile, parts, base)
        else:
            parts, base, terms = call(
                first_column_kernel, (part, line, tile_out), [wide], arrays=2
            )(tile, parts)
        parts = exchanged(parts, COL)
    core = place[4:5]

    def last(mine, skip, count, dtype):
        lines = jax.ShapeDtypeStruct((count // 128, 128), F32)
        spare = pltpu.VMEM((count, 128), F32)
        return call(
            functools.partial(last_kernel, mine, skip),
            (jax.ShapeDtypeStruct((count, FEATURES), dtype), lines, lines),
            [spare, spare, pltpu.VMEM((count, COLS), BF16)],
            count << 21,
            1,
            5,
        )(core, terms, tile, parts, base, block)

    away = last(False, 0, 512, BF16)
    other = [moved(value, "core", 1) for value in away]
    messages, skip = [], 0
    for count in OWN:
        own = last(True, skip, count, F32)
        message = call(
            functools.partial(cores_kernel, skip),
            jax.ShapeDtypeStruct((8, count // 128 * 134, 128), BF16),
            arrays=6,
        )(*own, *other)
        messages.append(exchanged(message, OWNERS))
        skip += count
    return call(
        groups_kernel, jax.ShapeDtypeStruct((512, 128), F32), arrays=len(messages)
    )(*messages)


OWN = (512,)
PACKS = ((0,), (1,), (7,), (2, 6), (3, 5), (4,))


def solution(mesh):
    torus = Mesh(mesh.devices.reshape(SIZES), AXES)
    rows = P(("y_hi", "z", "core"), ("y_lo", "x"))
    return jax.shard_map(
        local, mesh=torus, in_specs=(rows, P(AXES, None)), out_specs=rows, check_vma=False
    )
```

```python
import math

import jax
import jax.numpy as jnp
from jax import lax
from jax.experimental import pallas as pl
from jax.experimental.pallas import tpu as pltpu
from jax.sharding import Mesh
from jax.sharding import PartitionSpec as P


ITERS = 4
AXES = ("y_lo", "x", "y_hi", "z", "core")
SIZES = (2, 4, 2, 8, 2)
ROW = ("y_lo", "x", "core")
COL = ("y_hi", "z")
OWNERS = ("x", "y_lo")
BLOCKS = (0, 4, 1, 5, 2, 6, 3, 7)
FEATURES = 1024
ROWS = 1024
COLS = 1024
SAMPLES = 16384
STEP = 128
TINY = 2.0**-90
LARGE = 2.0**100
SHIFT = math.log2(SAMPLES)
SCALE = math.sqrt(FEATURES) * math.log2(math.e)
VMEM = pl.BlockSpec(memory_space=pltpu.VMEM)
SMEM = pl.BlockSpec(memory_space=pltpu.SMEM)
F32 = jnp.float32
BF16 = jnp.bfloat16


def call(kernel, out, scratch=(), flops=0, scalars=0, arrays=0, limit=8, aliases=None, kept=()):
    return pl.pallas_call(
        kernel,
        out_shape=out,
        in_specs=[
            pl.BlockSpec(memory_space=pl.ANY) if k in kept else SMEM if k < scalars else VMEM
            for k in range(scalars + arrays)
        ],
        out_specs=jax.tree.map(lambda _: VMEM, out),
        scratch_shapes=list(scratch),
        input_output_aliases=aliases or {},
        compiler_params=pltpu.CompilerParams(vmem_limit_bytes=limit << 20),
        cost_estimate=pl.CostEstimate(flops=flops, bytes_accessed=4 << 20, transcendentals=1 << 20),
    )


def diagonal():
    return lax.broadcasted_iota(jnp.int32, (128, 128), 0) == lax.broadcasted_iota(
        jnp.int32, (128, 128), 1
    )


def to_lanes(column, eye):
    parts = []
    for k in range(column.shape[0] // 128):
        spread = jnp.broadcast_to(column[k * 128 : (k + 1) * 128], (128, 128))
        parts.append(jnp.sum(jnp.where(eye, spread, 0.0), axis=0, keepdims=True))
    return jnp.concatenate(parts, axis=0)


def to_sublanes(line):
    return jnp.broadcast_to(line, (128, 128)).T


def joined_lse(parts):
    top = jnp.max(parts, axis=0)
    return top + jnp.log2(jnp.sum(jnp.exp2(parts - top[None]), axis=0))


def row_part(tile_ref, dual, out_ref, lse_ref):
    lines = [jnp.broadcast_to(dual[k : k + 1], (8, 128)) for k in range(8)]
    step = 64

    @pl.loop(0, ROWS // step)
    def _(at):
        rows = pl.ds(pl.multiple_of(at * step, step), step)
        logits = [
            tile_ref[rows, k * 128 : (k + 1) * 128] + jnp.tile(lines[k], (step // 8, 1))
            for k in range(8)
        ]
        top = logits[0]
        for part in logits[1:]:
            top = jnp.maximum(top, part)
        top = jnp.max(top, axis=1, keepdims=True)
        mass = jnp.exp2(logits[0] - top)
        for part in logits[1:]:
            mass = mass + jnp.exp2(part - top)
        mass = jnp.sum(mass, axis=1, keepdims=True)
        lse_ref[rows, :] = jnp.broadcast_to(top + jnp.log2(mass), (step, 128))

    out_ref[...] = jnp.broadcast_to(to_lanes(lse_ref[...], diagonal())[None], out_ref.shape)


def column_part(tile_ref, dual, out_ref, dual_ref):
    for k in range(8):
        dual_ref[k * 128 : (k + 1) * 128, :] = to_sublanes(dual[k : k + 1])
    step = 32

    def shifted(at, k):
        rows = pl.ds(pl.multiple_of(at * step, step), step)
        return tile_ref[rows, k * 128 : (k + 1) * 128] + dual_ref[rows, :]

    def peak(at, tops):
        return tuple(
            jnp.maximum(top, jnp.max(shifted(at, k).reshape(step // 8, 8, 128), axis=0))
            for k, top in enumerate(tops)
        )

    low = jnp.full((8, 128), -jnp.inf, F32)
    tops = lax.fori_loop(0, ROWS // step, peak, (low,) * 8)
    tops = [jnp.max(top, axis=0, keepdims=True) for top in tops]
    wide = [jnp.broadcast_to(top, (step, 128)) for top in tops]

    def add(at, sums):
        return tuple(
            total + jnp.sum(jnp.exp2(shifted(at, k) - wide[k]).reshape(step // 8, 8, 128), axis=0)
            for k, total in enumerate(sums)
        )

    sums = lax.fori_loop(0, ROWS // step, add, (jnp.zeros((8, 128), F32),) * 8)
    lse = jnp.concatenate(
        [
            top + jnp.log2(jnp.sum(total, axis=0, keepdims=True))
            for top, total in zip(tops, sums)
        ],
        axis=0,
    )
    out_ref[...] = jnp.broadcast_to(lse[None], out_ref.shape)


def lane_sums(wide):
    ones = jnp.ones((8, 128), BF16)
    rest, total = wide, 0.0
    for _ in range(3):
        piece = rest.astype(BF16)
        rest = rest - piece.astype(F32)
        total = total + lax.dot_general(
            ones, piece, (((1,), (1,)), ((), ())), preferred_element_type=F32
        )
    return jnp.concatenate(
        [total[0:1, k * 128 : (k + 1) * 128] for k in range(wide.shape[0] // 128)], axis=0
    )


def row_kernel(terms_ref, tile_ref, parts_ref, base_ref, out_ref, sums_ref):
    dual = -SHIFT - joined_lse(parts_ref[...])
    top = jnp.max(dual)
    factor = jnp.exp2(dual - top)
    lines = [jnp.broadcast_to(factor[k : k + 1], (8, 128)) for k in range(8)]

    @pl.loop(0, ROWS // STEP)
    def _(at):
        for q in range(STEP // 8):
            rows = pl.ds(pl.multiple_of(at * STEP + q * 8, 8), 8)
            mass = None
            for k in range(8):
                term = terms_ref[rows, k * 128 : (k + 1) * 128] * lines[k]
                mass = term if mass is None else mass + term
            sums_ref[rows, :] = mass

    total = lane_sums(sums_ref[...])
    lse = (top - SHIFT) - base_ref[...] + jnp.log2(total)
    out_ref[...] = jnp.broadcast_to(lse[None], out_ref.shape)

    @pl.when(jnp.min(total) < TINY)
    def _():
        row_part(tile_ref, dual, out_ref, sums_ref)


def column_total(sums):
    return jnp.concatenate([jnp.sum(part, axis=0, keepdims=True) for part in sums], axis=0)


def column_kernel(terms_ref, tile_ref, parts_ref, base_ref, out_ref, wide_ref):
    dual = -SHIFT - joined_lse(parts_ref[...])
    change = dual - base_ref[...]
    top = jnp.max(change)
    factor = jnp.exp2(change - top)
    for k in range(8):
        wide_ref[k * 128 : (k + 1) * 128, :] = to_sublanes(factor[k : k + 1])

    def add(at, sums):
        sums = list(sums)
        for q in range(STEP // 8):
            rows = pl.ds(pl.multiple_of(at * STEP + q * 8, 8), 8)
            share = wide_ref[rows, :]
            for k in range(8):
                sums[k] = sums[k] + terms_ref[rows, k * 128 : (k + 1) * 128] * share
        return tuple(sums)

    sums = lax.fori_loop(0, ROWS // STEP, add, (jnp.zeros((8, 128), F32),) * 8)
    total = column_total(sums)
    out_ref[...] = jnp.broadcast_to(((top - SHIFT) + jnp.log2(total))[None], out_ref.shape)

    @pl.when(jnp.min(total) < TINY)
    def _():
        column_part(tile_ref, dual, out_ref, wide_ref)


def first_column_kernel(tile_ref, parts_ref, out_ref, dual_ref, terms_ref, wide_ref):
    dual = -SHIFT - joined_lse(parts_ref[...])
    dual_ref[...] = dual
    for k in range(8):
        wide_ref[k * 128 : (k + 1) * 128, :] = to_sublanes(dual[k : k + 1] + SHIFT)

    def add(at, sums):
        sums = list(sums)
        for q in range(STEP // 8):
            rows = pl.ds(pl.multiple_of(at * STEP + q * 8, 8), 8)
            shift = wide_ref[rows, :]
            for k in range(8):
                here = slice(k * 128, (k + 1) * 128)
                term = jnp.exp2(tile_ref[rows, here] + shift)
                terms_ref[rows, here] = term
                sums[k] = sums[k] + term
        return tuple(sums)

    sums = lax.fori_loop(0, ROWS // STEP, add, (jnp.zeros((8, 128), F32),) * 8)
    total = column_total(sums)
    out_ref[...] = jnp.broadcast_to((jnp.log2(total) - SHIFT)[None], out_ref.shape)

    @pl.when(jnp.min(total) < TINY)
    def _():
        column_part(tile_ref, dual, out_ref, wide_ref)


def spread_kernel(noise_ref, other_ref, out_ref, sems):
    copies = [
        pltpu.make_async_copy(ref, out_ref.at[k, j], sems.at[k, j])
        for j, ref in enumerate((noise_ref, other_ref))
        for k in range(4)
    ]
    for copy in copies:
        copy.start()
    for copy in copies:
        copy.wait()


def pack_kernel(*refs):
    for k, ref in enumerate(refs[:-1]):
        refs[-1][k * 64 : (k + 1) * 64, :] = ref[...]


def squares(ref, rows):
    total = None
    for k in range(8):
        wide = ref[rows, k * 128 : (k + 1) * 128].astype(F32)
        total = wide * wide if total is None else total + wide * wide
    return jnp.sum(total, axis=1, keepdims=True)


def costs(rows_ref, block_ref, tile_ref, squares_ref, base, use):
    eye = diagonal()

    @pl.loop(0, 2)
    def _(at):
        cols = pl.ds(pl.multiple_of(base + at * 256, 256), 256)
        latent_sq = squares(block_ref, cols)
        cross = lax.dot_general(
            rows_ref[...], block_ref[cols, :], (((1,), (1,)), ((), ())), preferred_element_type=F32
        )
        pair = []
        for k in range(2):
            spread = jnp.broadcast_to(latent_sq[k * 128 : (k + 1) * 128], (128, 128))
            line = jnp.sum(jnp.where(eye, spread, 0.0), axis=0, keepdims=True)
            cost = squares_ref[...] + line - 2.0 * cross[:, k * 128 : (k + 1) * 128]
            cost = cost * (-SCALE / FEATURES)
            tile_ref[:, pl.ds(pl.multiple_of(base + at * 256 + k * 128, 128), 128)] = cost
            pair.append(cost)
        use(at, pair)


def placed(packs, block_ref, group, z, orders):
    for pack, backs in zip(packs, orders):
        for k, back in enumerate(backs):
            at = group * 8 + jnp.bitwise_and(z - back + 8, 7)
            rows = pl.ds(pl.multiple_of(at * 64, 64), 64)
            block_ref[rows, :] = pack[k * 64 : (k + 1) * 64, :]


def first_masses(tile_ref, base, top_ref, sums_ref):
    @pl.loop(0, ROWS // STEP)
    def _(at):
        for q in range(STEP // 8):
            rows = pl.ds(pl.multiple_of(at * STEP + q * 8, 8), 8)
            top = jnp.broadcast_to(jnp.max(top_ref[rows, :], axis=1, keepdims=True), (8, 128))
            top_ref[rows, :] = top
            mass = None
            for k in range(4):
                cols = pl.ds(pl.multiple_of(base + k * 128, 128), 128)
                term = jnp.exp2(tile_ref[rows, cols] - top)
                mass = term if mass is None else mass + term
            sums_ref[rows, :] = mass


def near_kernel(place_ref, *refs):
    noise, singles, near = refs[:2], refs[2:3], refs[3:7]
    rows_ref, block_ref, tile_ref, squares_ref, top_ref, sums_ref, line_ref, sems = refs[7:]
    y_lo, y_hi, z, core = (place_ref[k] for k in (0, 2, 3, 4))
    fetches = []
    for k, (single, backs) in enumerate(zip(singles, PACKS)):
        at = y_hi * 8 + jnp.bitwise_and(z - backs[0] + 8, 7)
        home = block_ref.at[pl.ds(pl.multiple_of(at * 64, 64), 64), :]
        fetches.append(pltpu.make_async_copy(single, home, sems.at[k]))
        fetches[-1].start()
    for half, ref in enumerate(noise):
        rows = pl.ds(pl.multiple_of(jnp.bitwise_xor(core, half) * 512, 512), 512)
        for k in range(4):
            for other in range(2):
                at = jnp.bitwise_xor(y_lo, other) * 4 + k
                rows_ref[rows, pl.ds(pl.multiple_of(at * 128, 128), 128)] = ref[k, other]
    placed(near, block_ref, y_hi, z, PACKS[1:])
    for k in range(8):
        rows = slice(k * 128, (k + 1) * 128)
        squares_ref[rows, :] = jnp.broadcast_to(squares(rows_ref, rows), (128, 128))
    for fetch in fetches:
        fetch.wait()
    base = pl.multiple_of(y_hi * 512, 512)

    def use(at, pair):
        top = jnp.maximum(*pair)
        top_ref[...] = jnp.maximum(jnp.where(at == 0, top, top_ref[...]), top)

    costs(rows_ref, block_ref, tile_ref, squares_ref, base, use)
    first_masses(tile_ref, base, top_ref, sums_ref)
    line_ref[...] = to_lanes(top_ref[...], diagonal())


def far_kernel(place_ref, rows_ref, *refs):
    far = refs[:5]
    squares_ref, top_ref, near_sums_ref, line_ref, _, _ = refs[5:11]
    block_ref, tile_ref, out_ref, sums_ref = refs[11:]
    y_hi, z = place_ref[2], place_ref[3]
    placed(far, block_ref, 1 - y_hi, z, PACKS)
    base = pl.multiple_of((1 - y_hi) * 512, 512)
    sums_ref[...] = near_sums_ref[...]

    def use(at, pair):
        top = top_ref[...]
        sums_ref[...] = sums_ref[...] + (jnp.exp2(pair[0] - top) + jnp.exp2(pair[1] - top))

    costs(rows_ref, block_ref, tile_ref, squares_ref, base, use)
    largest = jnp.max(sums_ref[...])
    lse = line_ref[...] + jnp.log2(lane_sums(sums_ref[...]))
    out_ref[...] = jnp.broadcast_to(lse[None], out_ref.shape)

    @pl.when(jnp.logical_not(largest < LARGE))
    def _():
        row_part(tile_ref, jnp.zeros((8, 128), F32), out_ref, sums_ref)


def away_kernel(
    core_ref, terms_ref, tile_ref, parts_ref, base_ref, block_ref,
    out_ref, limit_ref, mass_ref, own_ref, own_limit_ref, own_mass_ref,
    wide_ref, sums_ref, own_sums_ref, away_ref,
):
    dual = -SHIFT - joined_lse(parts_ref[...])
    top = jnp.max(dual)
    factor = jnp.exp2(dual - top)
    shares = [jnp.broadcast_to(factor[k : k + 1], (16, 128)) for k in range(8)]
    own = core_ref[0] * 512

    def keep(weights_ref, sums_ref, start, values):
        mass = None
        for k, term in enumerate(values):
            mass = term if mass is None else mass + term
            weights_ref[pl.ds(start, 16), k * 128 : (k + 1) * 128] = term.astype(BF16)
        sums_ref[pl.ds(start, 16), :] = mass

    def weigh(at, first, weights_ref, sums_ref):
        for q in range(8):
            start = pl.multiple_of(at * 128 + q * 16, 16)
            rows = pl.ds(pl.multiple_of(first + start, 16), 16)
            values = [terms_ref[rows, k * 128 : (k + 1) * 128] * shares[k] for k in range(8)]
            keep(weights_ref, sums_ref, start, values)

    def settle(first, weights_ref, sums_ref, limit_ref, mass_ref):
        base = jnp.where(first == 0, base_ref[0:4], base_ref[4:8])
        limit_ref[...] = (top - SHIFT) - base
        mass_ref[...] = lane_sums(sums_ref[...])

        @pl.when(jnp.min(mass_ref[...]) < TINY)
        def _():
            duals = [jnp.broadcast_to(dual[k : k + 1], (16, 128)) for k in range(8)]

            @pl.loop(0, 32)
            def _(at):
                start = pl.multiple_of(at * 16, 16)
                rows = pl.ds(pl.multiple_of(first + start, 16), 16)
                logits = [tile_ref[rows, k * 128 : (k + 1) * 128] + duals[k] for k in range(8)]
                peak = logits[0]
                for part in logits[1:]:
                    peak = jnp.maximum(peak, part)
                peak = jnp.broadcast_to(jnp.max(peak, axis=1, keepdims=True), (16, 128))
                wide_ref[pl.ds(start, 16), :] = peak
                keep(weights_ref, sums_ref, start, [jnp.exp2(part - peak) for part in logits])

            limit_ref[...] = to_lanes(wide_ref[...], diagonal())
            mass_ref[...] = lane_sums(sums_ref[...])

    @pl.loop(0, 4)
    def _(at):
        weigh(at, 512 - own, away_ref, sums_ref)

    settle(512 - own, away_ref, sums_ref, limit_ref, mass_ref)

    @pl.loop(0, 4)
    def _(at):
        here = pl.ds(pl.multiple_of(at * 256, 256), 256)
        weigh(at, own, own_ref, own_sums_ref)
        out_ref[:, here] = jnp.dot(
            away_ref[...], block_ref[:, here], preferred_element_type=F32
        ).astype(BF16)

    settle(own, own_ref, own_sums_ref, own_limit_ref, own_mass_ref)


def own_kernel(weights_ref, block_ref, out_ref):
    @pl.loop(0, 4)
    def _(at):
        here = pl.ds(pl.multiple_of(at * 256, 256), 256)
        out_ref[:, here] = jnp.dot(
            weights_ref[...], block_ref[:, here], preferred_element_type=F32
        )


def pieces_of(value):
    pieces = []
    for _ in range(3):
        pieces.append(value.astype(BF16))
        value = value - pieces[-1].astype(F32)
    return pieces


def cores_kernel(
    mine_ref, limit_ref, mass_ref, other_ref, other_limit_ref, other_mass_ref, out_ref
):
    limit = jnp.maximum(limit_ref[...], other_limit_ref[...])
    a, b = jnp.exp2(limit_ref[...] - limit), jnp.exp2(other_limit_ref[...] - limit)
    mass = a * mass_ref[...] + b * other_mass_ref[...]
    for k in range(4):
        wide_a, wide_b = to_sublanes(a[k : k + 1]), to_sublanes(b[k : k + 1])
        rows = slice(k * 128, (k + 1) * 128)
        for g, block in enumerate(BLOCKS):
            here = slice(block * 128, (block + 1) * 128)
            out_ref[g, rows, :] = (
                wide_a * mine_ref[rows, here] + wide_b * other_ref[rows, here].astype(F32)
            ).astype(BF16)
    pieces = jnp.concatenate(pieces_of(limit) + pieces_of(mass), axis=0)
    for g in range(8):
        out_ref[g, 512:, :] = pieces


def groups_kernel(*refs):
    out_ref, start = refs[-1], 0
    for parts_ref in refs[:-1]:
        count = parts_ref.shape[1] // 134 * 128
        n = count // 128
        pieces = parts_ref[:, count:, :].astype(F32)
        limit = pieces[:, 0:n] + pieces[:, n : 2 * n] + pieces[:, 2 * n : 3 * n]
        mass = pieces[:, 3 * n : 4 * n] + pieces[:, 4 * n : 5 * n] + pieces[:, 5 * n : 6 * n]
        share = jnp.exp2(limit - jnp.max(limit, axis=0)[None])
        share = share / jnp.sum(share * mass, axis=0)[None]
        for k in range(n):
            total = jnp.zeros((128, 128), F32)
            for g in range(8):
                total = total + to_sublanes(share[g, k : k + 1]) * parts_ref[
                    g, k * 128 : (k + 1) * 128, :
                ].astype(F32)
            out_ref[start + k * 128 : start + (k + 1) * 128, :] = total
        start += count


def moved(array, axis, step):
    size = lax.axis_size(axis)
    return lax.ppermute(array, axis, [(k, (k + step) % size) for k in range(size)])


def exchanged(parts, axes):
    return lax.all_to_all(parts, axes, 0, 0, tiled=True)


def local(noise_draws, latents):
    place = jnp.stack([lax.axis_index(axis) for axis in AXES]).astype(jnp.int32)
    part = jax.ShapeDtypeStruct((16, 8, 128), F32)
    line = jax.ShapeDtypeStruct((8, 128), F32)
    wide = pltpu.VMEM((ROWS, 128), F32)

    block_out = jax.ShapeDtypeStruct((COLS, FEATURES), BF16)
    tile_out = jax.ShapeDtypeStruct((ROWS, COLS), F32)
    wide_out = jax.ShapeDtypeStruct((ROWS, 128), F32)

    near, far = [latents] + [None] * 7, []
    near[1] = moved(latents, "z", 1)
    near[7] = moved(latents, "z", -1)
    near[2] = moved(near[1], "z", 1)
    near[6] = moved(near[7], "z", -1)
    near[3] = moved(near[2], "z", 1)
    near[5] = moved(near[6], "z", -1)
    near[4] = moved(near[2], "z", 2)
    packs = []
    for backs in PACKS:
        if len(backs) == 1:
            packs.append(near[backs[0]])
            continue
        packs.append(
            call(
                pack_kernel,
                jax.ShapeDtypeStruct((64 * len(backs), FEATURES), BF16),
                arrays=len(backs),
                limit=2,
            )(*(near[back] for back in backs))
        )
    far = [moved(pack, "y_hi", 1) for pack in packs]
    noise_pair = moved(noise_draws, "y_lo", 1)
    spread = pl.pallas_call(
        spread_kernel,
        out_shape=jax.ShapeDtypeStruct((4, 2, *noise_draws.shape), BF16),
        in_specs=[VMEM, VMEM],
        out_specs=pl.BlockSpec(memory_space=pl.ANY),
        scratch_shapes=[pltpu.SemaphoreType.DMA((4, 2))],
        name="spread",
        compiler_params=pltpu.CompilerParams(vmem_limit_bytes=2 << 20),
    )(noise_draws, noise_pair)
    features = exchanged(spread, "x")
    other_features = moved(features, "core", 1)
    rows, block, tile, squared, top, masses, peaks = call(
        near_kernel,
        (block_out, block_out, tile_out, wide_out, wide_out, wide_out, line),
        [pltpu.SemaphoreType.DMA((1,))],
        flops=1 << 30,
        scalars=1,
        arrays=7,
        kept=(3,),
    )(place, features, other_features, *packs)
    block, tile, parts = call(
        far_kernel, (block_out, tile_out, part), [wide], 1 << 30, 1, 12, aliases={11: 0, 12: 1}
    )(place, rows, *far, squared, top, masses, peaks, block, tile)
    for sweep in range(ITERS):
        if sweep:
            parts = call(row_kernel, part, [wide], arrays=4)(terms, tile, parts, base)
        parts = exchanged(parts, ROW)
        if sweep:
            parts = call(column_kernel, part, [wide], arrays=4)(terms, tile, parts, base)
        else:
            parts, base, terms = call(
                first_column_kernel, (part, line, tile_out), [wide], arrays=2
            )(tile, parts)
        parts = exchanged(parts, COL)
    core = place[4:5]

    half_lines = jax.ShapeDtypeStruct((4, 128), F32)
    half_wide = pltpu.VMEM((512, 128), F32)
    half_rows = jax.ShapeDtypeStruct((512, FEATURES), BF16)
    away, away_limit, away_mass, weights, limit, mass = call(
        away_kernel,
        (half_rows, half_lines, half_lines, half_rows, half_lines, half_lines),
        [half_wide, half_wide, half_wide, pltpu.VMEM((512, COLS), BF16)],
        1 << 30,
        1,
        5,
    )(core, terms, tile, parts, base, block)
    other = [moved(value, "core", 1) for value in (away, away_limit, away_mass)]
    own = call(
        own_kernel, jax.ShapeDtypeStruct((512, FEATURES), F32), flops=1 << 30, arrays=2
    )(weights, block)
    message = call(
        cores_kernel, jax.ShapeDtypeStruct((8, 536, 128), BF16), arrays=6
    )(own, limit, mass, *other)
    return call(groups_kernel, jax.ShapeDtypeStruct((512, 128), F32), arrays=1)(
        exchanged(message, OWNERS)
    )


PACKS = ((0,), (1, 7), (2, 6), (3, 5), (4,))


def solution(mesh):
    torus = Mesh(mesh.devices.reshape(SIZES), AXES)
    rows = P(("y_hi", "z", "core"), ("y_lo", "x"))
    return jax.shard_map(
        local, mesh=torus, in_specs=(rows, P(AXES, None)), out_specs=rows, check_vma=False
    )
```

```python
import math

import jax
import jax.numpy as jnp
from jax import lax
from jax.experimental import pallas as pl
from jax.experimental.pallas import tpu as pltpu
from jax.sharding import Mesh
from jax.sharding import PartitionSpec as P


ITERS = 4
AXES = ("y_lo", "x", "y_hi", "z", "core")
SIZES = (2, 4, 2, 8, 2)
ROW = ("y_lo", "x", "core")
COL = ("y_hi", "z")
OWNERS = ("x", "y_lo")
BLOCKS = (0, 4, 1, 5, 2, 6, 3, 7)
FEATURES = 1024
ROWS = 1024
COLS = 1024
SAMPLES = 16384
STEP = 128
TINY = 2.0**-90
LARGE = 2.0**100
SHIFT = math.log2(SAMPLES)
SCALE = math.sqrt(FEATURES) * math.log2(math.e)
VMEM = pl.BlockSpec(memory_space=pltpu.VMEM)
SMEM = pl.BlockSpec(memory_space=pltpu.SMEM)
F32 = jnp.float32
BF16 = jnp.bfloat16


def call(kernel, out, scratch=(), flops=0, scalars=0, arrays=0, limit=8, aliases=None, kept=()):
    return pl.pallas_call(
        kernel,
        out_shape=out,
        in_specs=[
            pl.BlockSpec(memory_space=pl.ANY) if k in kept else SMEM if k < scalars else VMEM
            for k in range(scalars + arrays)
        ],
        out_specs=jax.tree.map(lambda _: VMEM, out),
        scratch_shapes=list(scratch),
        input_output_aliases=aliases or {},
        compiler_params=pltpu.CompilerParams(vmem_limit_bytes=limit << 20),
        cost_estimate=pl.CostEstimate(flops=flops, bytes_accessed=4 << 20, transcendentals=1 << 20),
    )


def diagonal():
    return lax.broadcasted_iota(jnp.int32, (128, 128), 0) == lax.broadcasted_iota(
        jnp.int32, (128, 128), 1
    )


def to_lanes(column, eye):
    parts = []
    for k in range(column.shape[0] // 128):
        spread = jnp.broadcast_to(column[k * 128 : (k + 1) * 128], (128, 128))
        parts.append(jnp.sum(jnp.where(eye, spread, 0.0), axis=0, keepdims=True))
    return jnp.concatenate(parts, axis=0)


def to_sublanes(line):
    return jnp.broadcast_to(line, (128, 128)).T


def joined_lse(parts):
    top = jnp.max(parts, axis=0)
    return top + jnp.log2(jnp.sum(jnp.exp2(parts - top[None]), axis=0))


def row_part(tile_ref, dual, out_ref, lse_ref):
    lines = [jnp.broadcast_to(dual[k : k + 1], (8, 128)) for k in range(8)]
    step = 64

    @pl.loop(0, ROWS // step)
    def _(at):
        rows = pl.ds(pl.multiple_of(at * step, step), step)
        logits = [
            tile_ref[rows, k * 128 : (k + 1) * 128] + jnp.tile(lines[k], (step // 8, 1))
            for k in range(8)
        ]
        top = logits[0]
        for part in logits[1:]:
            top = jnp.maximum(top, part)
        top = jnp.max(top, axis=1, keepdims=True)
        mass = jnp.exp2(logits[0] - top)
        for part in logits[1:]:
            mass = mass + jnp.exp2(part - top)
        mass = jnp.sum(mass, axis=1, keepdims=True)
        lse_ref[rows, :] = jnp.broadcast_to(top + jnp.log2(mass), (step, 128))

    out_ref[...] = jnp.broadcast_to(to_lanes(lse_ref[...], diagonal())[None], out_ref.shape)


def column_part(tile_ref, dual, out_ref, dual_ref):
    for k in range(8):
        dual_ref[k * 128 : (k + 1) * 128, :] = to_sublanes(dual[k : k + 1])
    step = 32

    def shifted(at, k):
        rows = pl.ds(pl.multiple_of(at * step, step), step)
        return tile_ref[rows, k * 128 : (k + 1) * 128] + dual_ref[rows, :]

    def peak(at, tops):
        return tuple(
            jnp.maximum(top, jnp.max(shifted(at, k).reshape(step // 8, 8, 128), axis=0))
            for k, top in enumerate(tops)
        )

    low = jnp.full((8, 128), -jnp.inf, F32)
    tops = lax.fori_loop(0, ROWS // step, peak, (low,) * 8)
    tops = [jnp.max(top, axis=0, keepdims=True) for top in tops]
    wide = [jnp.broadcast_to(top, (step, 128)) for top in tops]

    def add(at, sums):
        return tuple(
            total + jnp.sum(jnp.exp2(shifted(at, k) - wide[k]).reshape(step // 8, 8, 128), axis=0)
            for k, total in enumerate(sums)
        )

    sums = lax.fori_loop(0, ROWS // step, add, (jnp.zeros((8, 128), F32),) * 8)
    lse = jnp.concatenate(
        [
            top + jnp.log2(jnp.sum(total, axis=0, keepdims=True))
            for top, total in zip(tops, sums)
        ],
        axis=0,
    )
    out_ref[...] = jnp.broadcast_to(lse[None], out_ref.shape)


def lane_sums(wide):
    ones = jnp.ones((8, 128), BF16)
    rest, total = wide, 0.0
    for _ in range(3):
        piece = rest.astype(BF16)
        rest = rest - piece.astype(F32)
        total = total + lax.dot_general(
            ones, piece, (((1,), (1,)), ((), ())), preferred_element_type=F32
        )
    return jnp.concatenate(
        [total[0:1, k * 128 : (k + 1) * 128] for k in range(wide.shape[0] // 128)], axis=0
    )


def row_kernel(terms_ref, tile_ref, parts_ref, base_ref, out_ref, sums_ref):
    dual = -SHIFT - joined_lse(parts_ref[...])
    top = jnp.max(dual)
    factor = jnp.exp2(dual - top)
    lines = [jnp.broadcast_to(factor[k : k + 1], (8, 128)) for k in range(8)]

    @pl.loop(0, ROWS // STEP)
    def _(at):
        for q in range(STEP // 8):
            rows = pl.ds(pl.multiple_of(at * STEP + q * 8, 8), 8)
            mass = None
            for k in range(8):
                term = terms_ref[rows, k * 128 : (k + 1) * 128] * lines[k]
                mass = term if mass is None else mass + term
            sums_ref[rows, :] = mass

    total = lane_sums(sums_ref[...])
    lse = (top - SHIFT) - base_ref[...] + jnp.log2(total)
    out_ref[...] = jnp.broadcast_to(lse[None], out_ref.shape)

    @pl.when(jnp.min(total) < TINY)
    def _():
        row_part(tile_ref, dual, out_ref, sums_ref)


def column_total(sums):
    return jnp.concatenate([jnp.sum(part, axis=0, keepdims=True) for part in sums], axis=0)


def column_kernel(terms_ref, tile_ref, parts_ref, base_ref, out_ref, wide_ref):
    dual = -SHIFT - joined_lse(parts_ref[...])
    change = dual - base_ref[...]
    top = jnp.max(change)
    factor = jnp.exp2(change - top)
    for k in range(8):
        wide_ref[k * 128 : (k + 1) * 128, :] = to_sublanes(factor[k : k + 1])

    def add(at, sums):
        sums = list(sums)
        for q in range(STEP // 8):
            rows = pl.ds(pl.multiple_of(at * STEP + q * 8, 8), 8)
            share = wide_ref[rows, :]
            for k in range(8):
                sums[k] = sums[k] + terms_ref[rows, k * 128 : (k + 1) * 128] * share
        return tuple(sums)

    sums = lax.fori_loop(0, ROWS // STEP, add, (jnp.zeros((8, 128), F32),) * 8)
    total = column_total(sums)
    out_ref[...] = jnp.broadcast_to(((top - SHIFT) + jnp.log2(total))[None], out_ref.shape)

    @pl.when(jnp.min(total) < TINY)
    def _():
        column_part(tile_ref, dual, out_ref, wide_ref)


def first_column_kernel(tile_ref, parts_ref, out_ref, dual_ref, terms_ref, wide_ref):
    dual = -SHIFT - joined_lse(parts_ref[...])
    dual_ref[...] = dual
    for k in range(8):
        wide_ref[k * 128 : (k + 1) * 128, :] = to_sublanes(dual[k : k + 1] + SHIFT)

    def add(at, sums):
        sums = list(sums)
        for q in range(STEP // 8):
            rows = pl.ds(pl.multiple_of(at * STEP + q * 8, 8), 8)
            shift = wide_ref[rows, :]
            for k in range(8):
                here = slice(k * 128, (k + 1) * 128)
                term = jnp.exp2(tile_ref[rows, here] + shift)
                terms_ref[rows, here] = term
                sums[k] = sums[k] + term
        return tuple(sums)

    sums = lax.fori_loop(0, ROWS // STEP, add, (jnp.zeros((8, 128), F32),) * 8)
    total = column_total(sums)
    out_ref[...] = jnp.broadcast_to((jnp.log2(total) - SHIFT)[None], out_ref.shape)

    @pl.when(jnp.min(total) < TINY)
    def _():
        column_part(tile_ref, dual, out_ref, wide_ref)


def spread_kernel(noise_ref, other_ref, out_ref, sems):
    copies = [
        pltpu.make_async_copy(ref, out_ref.at[k, j], sems.at[k, j])
        for j, ref in enumerate((noise_ref, other_ref))
        for k in range(4)
    ]
    for copy in copies:
        copy.start()
    for copy in copies:
        copy.wait()


def pack_kernel(*refs):
    for k, ref in enumerate(refs[:-1]):
        refs[-1][k * 64 : (k + 1) * 64, :] = ref[...]


def squares(ref, rows):
    total = None
    for k in range(8):
        wide = ref[rows, k * 128 : (k + 1) * 128].astype(F32)
        total = wide * wide if total is None else total + wide * wide
    return jnp.sum(total, axis=1, keepdims=True)


def costs(rows_ref, block_ref, tile_ref, squares_ref, base, use):
    eye = diagonal()

    @pl.loop(0, 2)
    def _(at):
        cols = pl.ds(pl.multiple_of(base + at * 256, 256), 256)
        latent_sq = squares(block_ref, cols)
        cross = lax.dot_general(
            rows_ref[...], block_ref[cols, :], (((1,), (1,)), ((), ())), preferred_element_type=F32
        )
        pair = []
        for k in range(2):
            spread = jnp.broadcast_to(latent_sq[k * 128 : (k + 1) * 128], (128, 128))
            line = jnp.sum(jnp.where(eye, spread, 0.0), axis=0, keepdims=True)
            cost = squares_ref[...] + line - 2.0 * cross[:, k * 128 : (k + 1) * 128]
            cost = cost * (-SCALE / FEATURES)
            tile_ref[:, pl.ds(pl.multiple_of(base + at * 256 + k * 128, 128), 128)] = cost
            pair.append(cost)
        use(at, pair)


def placed(packs, block_ref, group, z, orders):
    for pack, backs in zip(packs, orders):
        for k, back in enumerate(backs):
            at = group * 8 + jnp.bitwise_and(z - back + 8, 7)
            rows = pl.ds(pl.multiple_of(at * 64, 64), 64)
            block_ref[rows, :] = pack[k * 64 : (k + 1) * 64, :]


def near_kernel(place_ref, *refs):
    noise, singles, near = refs[:2], refs[2:3], refs[3:7]
    rows_ref, block_ref, tile_ref, squares_ref, top_ref, sums_ref, line_ref, sems = refs[7:]
    y_lo, y_hi, z, core = (place_ref[k] for k in (0, 2, 3, 4))
    fetches = []
    for k, (single, backs) in enumerate(zip(singles, PACKS)):
        at = y_hi * 8 + jnp.bitwise_and(z - backs[0] + 8, 7)
        home = block_ref.at[pl.ds(pl.multiple_of(at * 64, 64), 64), :]
        fetches.append(pltpu.make_async_copy(single, home, sems.at[k]))
        fetches[-1].start()
    for half, ref in enumerate(noise):
        rows = pl.ds(pl.multiple_of(jnp.bitwise_xor(core, half) * 512, 512), 512)
        for k in range(4):
            for other in range(2):
                at = jnp.bitwise_xor(y_lo, other) * 4 + k
                rows_ref[rows, pl.ds(pl.multiple_of(at * 128, 128), 128)] = ref[k, other]
    placed(near, block_ref, y_hi, z, PACKS[1:])
    for k in range(8):
        rows = slice(k * 128, (k + 1) * 128)
        squares_ref[rows, :] = jnp.broadcast_to(squares(rows_ref, rows), (128, 128))
    for fetch in fetches:
        fetch.wait()
    base = pl.multiple_of(y_hi * 512, 512)

    def use(at, pair):
        @pl.when(at == 0)
        def _():
            peak = jnp.max(jnp.maximum(*pair), axis=1, keepdims=True)
            top_ref[...] = jnp.broadcast_to(peak, (ROWS, 128))
            sums_ref[...] = jnp.zeros((ROWS, 128), F32)

        top = top_ref[...]
        sums_ref[...] = sums_ref[...] + (jnp.exp2(pair[0] - top) + jnp.exp2(pair[1] - top))

    costs(rows_ref, block_ref, tile_ref, squares_ref, base, use)
    line_ref[...] = to_lanes(top_ref[...], diagonal())


def far_kernel(place_ref, rows_ref, *refs):
    far = refs[:5]
    squares_ref, top_ref, near_sums_ref, line_ref, _, _ = refs[5:11]
    block_ref, tile_ref, out_ref, sums_ref = refs[11:]
    y_hi, z = place_ref[2], place_ref[3]
    placed(far, block_ref, 1 - y_hi, z, PACKS)
    base = pl.multiple_of((1 - y_hi) * 512, 512)
    sums_ref[...] = near_sums_ref[...]

    def use(at, pair):
        top = top_ref[...]
        sums_ref[...] = sums_ref[...] + (jnp.exp2(pair[0] - top) + jnp.exp2(pair[1] - top))

    costs(rows_ref, block_ref, tile_ref, squares_ref, base, use)
    largest = jnp.max(sums_ref[...])
    lse = line_ref[...] + jnp.log2(lane_sums(sums_ref[...]))
    out_ref[...] = jnp.broadcast_to(lse[None], out_ref.shape)

    @pl.when(jnp.logical_not(largest < LARGE))
    def _():
        row_part(tile_ref, jnp.zeros((8, 128), F32), out_ref, sums_ref)


def away_kernel(
    core_ref, terms_ref, tile_ref, parts_ref, base_ref, block_ref,
    out_ref, limit_ref, mass_ref, own_ref, own_limit_ref, own_mass_ref,
    wide_ref, sums_ref, own_sums_ref, away_ref,
):
    dual = -SHIFT - joined_lse(parts_ref[...])
    top = jnp.max(dual)
    factor = jnp.exp2(dual - top)
    shares = [jnp.broadcast_to(factor[k : k + 1], (16, 128)) for k in range(8)]
    own = core_ref[0] * 512

    def keep(weights_ref, sums_ref, start, values):
        mass = None
        for k, term in enumerate(values):
            mass = term if mass is None else mass + term
            weights_ref[pl.ds(start, 16), k * 128 : (k + 1) * 128] = term.astype(BF16)
        sums_ref[pl.ds(start, 16), :] = mass

    def weigh(at, first, weights_ref, sums_ref):
        for q in range(8):
            start = pl.multiple_of(at * 128 + q * 16, 16)
            rows = pl.ds(pl.multiple_of(first + start, 16), 16)
            values = [terms_ref[rows, k * 128 : (k + 1) * 128] * shares[k] for k in range(8)]
            keep(weights_ref, sums_ref, start, values)

    def settle(first, weights_ref, sums_ref, limit_ref, mass_ref):
        base = jnp.where(first == 0, base_ref[0:4], base_ref[4:8])
        limit_ref[...] = (top - SHIFT) - base
        mass_ref[...] = lane_sums(sums_ref[...])

        @pl.when(jnp.min(mass_ref[...]) < TINY)
        def _():
            duals = [jnp.broadcast_to(dual[k : k + 1], (16, 128)) for k in range(8)]

            @pl.loop(0, 32)
            def _(at):
                start = pl.multiple_of(at * 16, 16)
                rows = pl.ds(pl.multiple_of(first + start, 16), 16)
                logits = [tile_ref[rows, k * 128 : (k + 1) * 128] + duals[k] for k in range(8)]
                peak = logits[0]
                for part in logits[1:]:
                    peak = jnp.maximum(peak, part)
                peak = jnp.broadcast_to(jnp.max(peak, axis=1, keepdims=True), (16, 128))
                wide_ref[pl.ds(start, 16), :] = peak
                keep(weights_ref, sums_ref, start, [jnp.exp2(part - peak) for part in logits])

            limit_ref[...] = to_lanes(wide_ref[...], diagonal())
            mass_ref[...] = lane_sums(sums_ref[...])

    @pl.loop(0, 4)
    def _(at):
        weigh(at, 512 - own, away_ref, sums_ref)

    settle(512 - own, away_ref, sums_ref, limit_ref, mass_ref)

    @pl.loop(0, 4)
    def _(at):
        here = pl.ds(pl.multiple_of(at * 256, 256), 256)
        weigh(at, own, own_ref, own_sums_ref)
        out_ref[:, here] = jnp.dot(
            away_ref[...], block_ref[:, here], preferred_element_type=F32
        ).astype(BF16)

    settle(own, own_ref, own_sums_ref, own_limit_ref, own_mass_ref)


def own_kernel(weights_ref, block_ref, out_ref):
    @pl.loop(0, 4)
    def _(at):
        here = pl.ds(pl.multiple_of(at * 256, 256), 256)
        out_ref[:, here] = jnp.dot(
            weights_ref[...], block_ref[:, here], preferred_element_type=F32
        )


def pieces_of(value):
    pieces = []
    for _ in range(3):
        pieces.append(value.astype(BF16))
        value = value - pieces[-1].astype(F32)
    return pieces


def cores_kernel(
    mine_ref, limit_ref, mass_ref, other_ref, other_limit_ref, other_mass_ref, out_ref
):
    limit = jnp.maximum(limit_ref[...], other_limit_ref[...])
    a, b = jnp.exp2(limit_ref[...] - limit), jnp.exp2(other_limit_ref[...] - limit)
    mass = a * mass_ref[...] + b * other_mass_ref[...]
    for k in range(4):
        wide_a, wide_b = to_sublanes(a[k : k + 1]), to_sublanes(b[k : k + 1])
        rows = slice(k * 128, (k + 1) * 128)
        for g, block in enumerate(BLOCKS):
            here = slice(block * 128, (block + 1) * 128)
            out_ref[g, rows, :] = (
                wide_a * mine_ref[rows, here] + wide_b * other_ref[rows, here].astype(F32)
            ).astype(BF16)
    pieces = jnp.concatenate(pieces_of(limit) + pieces_of(mass), axis=0)
    for g in range(8):
        out_ref[g, 512:, :] = pieces


def groups_kernel(*refs):
    out_ref, start = refs[-1], 0
    for parts_ref in refs[:-1]:
        count = parts_ref.shape[1] // 134 * 128
        n = count // 128
        pieces = parts_ref[:, count:, :].astype(F32)
        limit = pieces[:, 0:n] + pieces[:, n : 2 * n] + pieces[:, 2 * n : 3 * n]
        mass = pieces[:, 3 * n : 4 * n] + pieces[:, 4 * n : 5 * n] + pieces[:, 5 * n : 6 * n]
        share = jnp.exp2(limit - jnp.max(limit, axis=0)[None])
        share = share / jnp.sum(share * mass, axis=0)[None]
        for k in range(n):
            total = jnp.zeros((128, 128), F32)
            for g in range(8):
                total = total + to_sublanes(share[g, k : k + 1]) * parts_ref[
                    g, k * 128 : (k + 1) * 128, :
                ].astype(F32)
            out_ref[start + k * 128 : start + (k + 1) * 128, :] = total
        start += count


def moved(array, axis, step):
    size = lax.axis_size(axis)
    return lax.ppermute(array, axis, [(k, (k + step) % size) for k in range(size)])


def exchanged(parts, axes):
    return lax.all_to_all(parts, axes, 0, 0, tiled=True)


def local(noise_draws, latents):
    place = jnp.stack([lax.axis_index(axis) for axis in AXES]).astype(jnp.int32)
    part = jax.ShapeDtypeStruct((16, 8, 128), F32)
    line = jax.ShapeDtypeStruct((8, 128), F32)
    wide = pltpu.VMEM((ROWS, 128), F32)

    block_out = jax.ShapeDtypeStruct((COLS, FEATURES), BF16)
    tile_out = jax.ShapeDtypeStruct((ROWS, COLS), F32)
    wide_out = jax.ShapeDtypeStruct((ROWS, 128), F32)

    near, far = [latents] + [None] * 7, []
    near[1] = moved(latents, "z", 1)
    near[7] = moved(latents, "z", -1)
    near[2] = moved(near[1], "z", 1)
    near[6] = moved(near[7], "z", -1)
    near[3] = moved(near[2], "z", 1)
    near[5] = moved(near[6], "z", -1)
    near[4] = moved(near[2], "z", 2)
    packs = []
    for backs in PACKS:
        if len(backs) == 1:
            packs.append(near[backs[0]])
            continue
        packs.append(
            call(
                pack_kernel,
                jax.ShapeDtypeStruct((64 * len(backs), FEATURES), BF16),
                arrays=len(backs),
                limit=2,
            )(*(near[back] for back in backs))
        )
    far = [moved(pack, "y_hi", 1) for pack in packs]
    noise_pair = moved(noise_draws, "y_lo", 1)
    spread = pl.pallas_call(
        spread_kernel,
        out_shape=jax.ShapeDtypeStruct((4, 2, *noise_draws.shape), BF16),
        in_specs=[VMEM, VMEM],
        out_specs=pl.BlockSpec(memory_space=pl.ANY),
        scratch_shapes=[pltpu.SemaphoreType.DMA((4, 2))],
        name="spread",
        compiler_params=pltpu.CompilerParams(vmem_limit_bytes=2 << 20),
    )(noise_draws, noise_pair)
    features = exchanged(spread, "x")
    other_features = moved(features, "core", 1)
    rows, block, tile, squared, top, masses, peaks = call(
        near_kernel,
        (block_out, block_out, tile_out, wide_out, wide_out, wide_out, line),
        [pltpu.SemaphoreType.DMA((1,))],
        flops=1 << 30,
        scalars=1,
        arrays=7,
        kept=(3,),
    )(place, features, other_features, *packs)
    block, tile, parts = call(
        far_kernel, (block_out, tile_out, part), [wide], 1 << 30, 1, 12, aliases={11: 0, 12: 1}
    )(place, rows, *far, squared, top, masses, peaks, block, tile)
    for sweep in range(ITERS):
        if sweep:
            parts = call(row_kernel, part, [wide], arrays=4)(terms, tile, parts, base)
        parts = exchanged(parts, ROW)
        if sweep:
            parts = call(column_kernel, part, [wide], arrays=4)(terms, tile, parts, base)
        else:
            parts, base, terms = call(
                first_column_kernel, (part, line, tile_out), [wide], arrays=2
            )(tile, parts)
        parts = exchanged(parts, COL)
    core = place[4:5]

    half_lines = jax.ShapeDtypeStruct((4, 128), F32)
    half_wide = pltpu.VMEM((512, 128), F32)
    half_rows = jax.ShapeDtypeStruct((512, FEATURES), BF16)
    away, away_limit, away_mass, weights, limit, mass = call(
        away_kernel,
        (half_rows, half_lines, half_lines, half_rows, half_lines, half_lines),
        [half_wide, half_wide, half_wide, pltpu.VMEM((512, COLS), BF16)],
        1 << 30,
        1,
        5,
    )(core, terms, tile, parts, base, block)
    other = [moved(value, "core", 1) for value in (away, away_limit, away_mass)]
    own = call(
        own_kernel, jax.ShapeDtypeStruct((512, FEATURES), F32), flops=1 << 30, arrays=2
    )(weights, block)
    message = call(
        cores_kernel, jax.ShapeDtypeStruct((8, 536, 128), BF16), arrays=6
    )(own, limit, mass, *other)
    return call(groups_kernel, jax.ShapeDtypeStruct((512, 128), F32), arrays=1)(
        exchanged(message, OWNERS)
    )


PACKS = ((0,), (1, 7), (2, 6), (3, 5), (4,))


def solution(mesh):
    torus = Mesh(mesh.devices.reshape(SIZES), AXES)
    rows = P(("y_hi", "z", "core"), ("y_lo", "x"))
    return jax.shard_map(
        local, mesh=torus, in_specs=(rows, P(AXES, None)), out_specs=rows, check_vma=False
    )
```
